128 devices in a mesh: gx: 32 (over y_lo, x, z), gy: 4 (over y_hi, core).
Axes of the slice: x: 4, y: 4 (y_hi: 2, y_lo: 2; y = y_hi * 2 + y_lo), z: 4, core: 2. Of those that a mesh axis runs over, the one named last changes fastest.
Arguments:
- orbitals: float32 [32, 256, 32, 128], P(None, 'gx', 'gy'), may hold values from -340 to 340
- potential: float32 [256, 32, 128], P('gx', 'gy'), may hold values from -3 to 1
Outputs:
- orthonormal: float32 [32, 256, 32, 128], P(None, 'gx', 'gy')
- rfactor: float32 [32, 32], replicated
The draws below stay inside these ranges and needn't reach their ends.
All inputs are finite; a program needn't handle non-finite values.
Results may differ from the reference program's by a relative error of at most 0.0003.
Values sent between devices are 32-bit elements; how exact they have to be, the bound alone decides.
No kernel may reach another device: no remote copies, remote signals or barrier semaphores. Data moves between devices by JAX's collectives and lax.ppermute only.
A program may use at most 128 MiB of HBM per device.

```python
import math
import jax
import jax.numpy as jnp
from jax import lax

NORB = 32
DEGREE = 3
CZ = 128
NX = 256
NY = 32
N_GX = 32
N_GY = 4


def draw_orbitals(key, part):
    subkeys = jax.random.split(key, 3)
    full_shape = (NORB, NX, NY, CZ)
    along_x = 1.0 + 2.0 * jnp.arange(NX, dtype=jnp.float32)[:, None, None] / max(NX - 1, 1)
    cell_scale = jnp.exp(jax.random.uniform(subkeys[1], (NX, NY, CZ), minval=math.log(0.3), maxval=math.log(3.0)))
    orbital_scale = jnp.exp(jax.random.uniform(subkeys[2], (NORB, 1, 1, 1), minval=math.log(0.3), maxval=math.log(3.0)))
    sample_values = jnp.clip(jax.random.normal(subkeys[0], full_shape), -6.0, 6.0)
    envelope = cell_scale * along_x
    return (sample_values * envelope[None] * orbital_scale).astype(jnp.float32)


def block_scale(own_key, shape, pieces, low, top_value):
    factor_of = 1.0
    for position, shards_of in pieces:
        steps = jax.random.uniform(jax.random.fold_in(jax.random.fold_in(own_key, 6), position), (shards_of,), jnp.float32, low / len(pieces), top_value / len(pieces))
        factor_of = factor_of * jnp.repeat(jnp.exp(steps), shape[position] // shards_of).reshape((-1,) + (1,) * (len(shape) - 1 - position))
    return factor_of


def setup_inputs(seed: int = 0) -> dict:
    key_of = jax.random.split(jax.random.key(seed), 3)
    return {
        "orbitals": draw_orbitals(jax.random.fold_in(key_of[2], 71), 0),
        "potential": jnp.clip(-3.0 + 4.0 * jax.random.uniform(key_of[1], (NX, NY, CZ), jnp.float32) ** block_scale(key_of[1], (NX, NY, CZ), ((0, 32), (1, 4)), -0.2, 0.2), -3.0, 1.0),
    }


stencil_weights = (-5369.0 / 1800.0, 12.0 / 7.0, -15.0 / 56.0, 10.0 / 189.0, -1.0 / 112.0, 2.0 / 1925.0, -1.0 / 16632.0)
grid_spacing = 0.5
filter_low = 4.0
filter_high = 46.0

def scaled_apply(orbital_field, potential):
    laplace = 3.0 * stencil_weights[0] * orbital_field
    for offset in range(1, 7):
        for axis_pos in range(3):
            laplace = laplace + stencil_weights[offset] * (jnp.roll(orbital_field, offset, axis_pos) + jnp.roll(orbital_field, -offset, axis_pos))
    applied = -0.5 / grid_spacing ** 2 * laplace + potential * orbital_field
    centre_shift = 0.5 * (filter_high + filter_low)
    half_width = 0.5 * (filter_high - filter_low)
    return (applied - centre_shift * orbital_field) / half_width

def reference(orbitals, potential):

    def filter_one(orbital_field):
        previous = orbital_field
        current = scaled_apply(orbital_field, potential)
        for degree_step in range(DEGREE - 1):
            following = 2.0 * scaled_apply(current, potential) - previous
            previous, current = (current, following)
        return current
    filtered = lax.map(filter_one, orbitals)
    cell_count = NX * NY * CZ
    matrix = filtered.reshape(NORB, cell_count)
    block_count = N_GX * N_GY
    blocks = matrix.reshape(NORB, block_count, cell_count // block_count).transpose(1, 2, 0)
    partial_r = lax.map(lambda block_rows: jnp.linalg.qr(block_rows, mode='r'), blocks)
    combined = jnp.linalg.qr(partial_r.reshape(block_count * NORB, NORB), mode='r')
    signs = jnp.where(jnp.diagonal(combined) >= 0, 1.0, -1.0).astype(combined.dtype)
    rfactor = combined * signs[:, None] / math.sqrt(cell_count)
    basis_rows = jax.scipy.linalg.solve_triangular(rfactor.T, matrix, lower=True)
    return (basis_rows.reshape(NORB, NX, NY, CZ), rfactor)
```

```python
import functools

import jax
import jax.numpy as jnp
from jax import lax
from jax.experimental import pallas as pl
from jax.experimental.pallas import tpu as pltpu
from jax.sharding import Mesh
from jax.sharding import PartitionSpec as P

stencil_weights = (
    -5369.0 / 1800.0,
    12.0 / 7.0,
    -15.0 / 56.0,
    10.0 / 189.0,
    -1.0 / 112.0,
    2.0 / 1925.0,
    -1.0 / 16632.0,
)
grid_spacing = 0.5
filter_low = 4.0
filter_high = 46.0
centre_shift = 0.5 * (filter_high + filter_low)
half_width = 0.5 * (filter_high - filter_low)
kinetic = -0.5 / grid_spacing**2
diagonal = (kinetic * 3.0 * stencil_weights[0] - centre_shift) / half_width
coupling = tuple(kinetic * w / half_width for w in stencil_weights)
highest = lax.Precision.HIGHEST

REACH = 6
DEEP = 3 * REACH
FLAT = 2 * REACH
PAIR = 2
BX = 8
SLAB = 4 * BX
VMEM = pl.BlockSpec(memory_space=pltpu.VMEM)
SMEM = pl.BlockSpec(memory_space=pltpu.SMEM)


def pack_kernel(got, up, down):
    for dest, first, first_flat in ((up, SLAB - DEEP, SLAB - FLAT), (down, 0, 0)):
        for o in range(PAIR):
            for i in range(DEEP):
                z, xi = divmod(first + i, BX)
                for gy in range(4):
                    dest[o * DEEP + i, gy] = got[z * 4 + gy, o * BX + xi]
        for i in range(FLAT // 2):
            z, xi = divmod(first_flat // 2 + i, BX // 2)
            for gy in range(4):
                dest[PAIR * DEEP + i, gy] = got[z * 4 + gy, PAIR * BX + xi]


def filter_kernel(core, got, low, high, far, far_low, far_high, out, field0, field1, field2, pot):
    mine = core[0]

    def put(field, o, row, tiles):
        for t in range(4):
            field[o, row, 8 + 8 * t : 16 + 8 * t] = tiles[t]
        field[o, row, 0:8] = tiles[3]
        field[o, row, 40:48] = tiles[0]

    for o in range(PAIR):
        def edge(i, carry, o=o):
            put(field0, o, i, [low[o * DEEP + i, gy] for gy in range(4)])
            put(field0, o, DEEP + SLAB + i, [high[o * DEEP + i, gy] for gy in range(4)])
            return carry

        lax.fori_loop(0, DEEP, edge, 0)
        for z in range(4):
            def inner(xi, carry, o=o, z=z):
                put(field0, o, DEEP + z * BX + xi, [got[z * 4 + gy, o * BX + xi] for gy in range(4)])
                return carry

            lax.fori_loop(0, BX, inner, 0)

    def put_pot(row, own, other):
        for gy in range(4):
            pot[row + mine, 8 * gy : 8 * gy + 8] = diagonal + own[gy] * (1.0 / half_width)
            pot[row + 1 - mine, 8 * gy : 8 * gy + 8] = diagonal + other[gy] * (1.0 / half_width)

    for i in range(FLAT // 2):
        r = PAIR * DEEP + i
        put_pot(2 * i, [low[r, g] for g in range(4)], [far_low[i, g] for g in range(4)])
        put_pot(
            FLAT + SLAB + 2 * i, [high[r, g] for g in range(4)], [far_high[i, g] for g in range(4)]
        )
    for z in range(4):
        for i in range(BX // 2):
            put_pot(
                FLAT + z * BX + 2 * i,
                [got[z * 4 + g, PAIR * BX + i] for g in range(4)],
                [far[z * 4 + g, i] for g in range(4)],
            )

    def apply(field, o, row, pot_row):
        v = field[o, row, 8:40]
        total = pot[pot_row] * v
        for j in range(1, REACH + 1):
            near = (field[o, row + j, 8:40] + field[o, row - j, 8:40]) + (
                field[o, row, 8 + j : 40 + j] + field[o, row, 8 - j : 40 - j]
            )
            near = near + (pltpu.roll(v, j, 1) + pltpu.roll(v, 128 - j, 1))
            total = total + coupling[j] * near
        return total

    def tiles_of(t):
        return [t[8 * k : 8 * k + 8] for k in range(4)]

    def first(i, carry):
        for o in range(PAIR):
            put(field1, o, i, tiles_of(apply(field0, o, i + REACH, i)))
        return carry

    lax.fori_loop(0, SLAB + 2 * FLAT, first, 0)

    def second(i, carry):
        for o in range(PAIR):
            t = apply(field1, o, i + REACH, i + REACH)
            put(field2, o, i, tiles_of(t + t - field0[o, i + FLAT, 8:40]))
        return carry

    lax.fori_loop(0, SLAB + FLAT, second, 0)

    for z in range(4):
        def third(xi, carry, z=z):
            i = z * BX + xi
            for o in range(PAIR):
                t = apply(field2, o, i + REACH, i + FLAT)
                t = t + t - field1[o, i + FLAT, 8:40]
                for gy in range(4):
                    out[z * 4 + gy, o, xi] = t[8 * gy : 8 * gy + 8]
            return carry

        lax.fori_loop(0, BX, third, 0)


def iota(shape, dim):
    return lax.broadcasted_iota(jnp.int32, shape, dim)


def spread(orbital_count):
    shape = (orbital_count * BX, orbital_count)
    return (iota(shape, 0) // BX == iota(shape, 1)).astype(jnp.float32)


def same_y(orbital_count):
    shape = (orbital_count * BX, orbital_count * BX)
    return iota(shape, 0) % BX == iota(shape, 1) % BX


def dot(a, b, dims=((1,), (0,))):
    return lax.dot_general(
        a, b, (dims, ((), ())), precision=highest, preferred_element_type=jnp.float32
    )


def gram_kernel(scale, y, out):
    n = y.shape[0]
    total = None
    for x in range(BX):
        block = y[:, x].reshape(n * BX, 128)
        part = dot(block, block, ((1,), (1,)))
        total = part if total is None else total + part
    total = jnp.where(same_y(n), total, 0.0) * scale
    ones = spread(n)
    gram = dot(dot(ones, total, ((0,), (0,))), ones)
    wide = jnp.concatenate([gram[8 * k : 8 * k + 8] for k in range(n // 8)], axis=1)
    for d in range(out.shape[0]):
        out[d] = wide


def finish_kernel(parts, y, out, factor):
    n = y.shape[0]
    wide = jnp.sum(parts[...], axis=0)
    gram = jnp.concatenate([wide[:, n * k : n * k + n] for k in range(n // 8)], axis=0)
    unit = (iota((n, n), 0) == iota((n, n), 1)).astype(jnp.float32)
    left = jnp.concatenate([gram, unit, jnp.zeros((n, 128 - 2 * n), jnp.float32)], axis=1)
    row_of = iota((n, 128), 0)
    done = jnp.zeros((n, 128), jnp.float32)
    for k in range(n):
        inverse = lax.rsqrt(left[k : k + 1, k : k + 1])
        row = left[k : k + 1] * inverse
        column = left[:, k : k + 1] * inverse
        done = jnp.where(row_of == k, row, done)
        left = left - jnp.where(row_of > k, column, 0.0) * row
    factor[...] = jnp.where(iota((n, n), 0) <= iota((n, n), 1), done[:, :n], 0.0)
    mixer = done[:, n : 2 * n]
    ones = spread(n)
    wide_mixer = jnp.where(same_y(n), dot(dot(ones, mixer), ones, ((1,), (1,))), 0.0)
    for x in range(BX):
        block = y[:, x].reshape(n * BX, 128)
        out[:, x] = dot(wide_mixer, block).reshape(n, BX, 128)


def call(kernel, out_shape, in_specs, scratch=(), flops=0, moved=0):
    return pl.pallas_call(
        kernel,
        out_shape=out_shape,
        in_specs=in_specs,
        out_specs=jax.tree.map(lambda _: VMEM, out_shape),
        scratch_shapes=list(scratch),
        cost_estimate=pl.CostEstimate(flops=flops, bytes_accessed=moved, transcendentals=0),
    )


def f32(*shape):
    return jax.ShapeDtypeStruct(shape, jnp.float32)


def per_device(orbitals, potential):
    n = orbitals.shape[0]
    slabs = lax.axis_size("s")
    group = lax.axis_size("z") * lax.axis_size("gy")
    core = lax.axis_index("gy") % 2
    halves = potential.reshape(BX // 2, 2, BX, 128).swapaxes(0, 1)
    halves = jnp.broadcast_to(halves[None], (group // 2, 2, BX // 2, BX, 128))
    sent = jnp.concatenate(
        [orbitals.reshape(group, PAIR * BX, BX, 128), halves.reshape(group, BX // 2, BX, 128)],
        axis=1,
    )
    got = lax.all_to_all(sent, ("z", "gy"), 0, 0, tiled=True)
    rows = PAIR * DEEP + FLAT // 2
    up, down = call(pack_kernel, (f32(rows, 4, 8, 128),) * 2, [VMEM])(got)
    ring = [(i, (i + 1) % slabs) for i in range(slabs)]
    low = lax.ppermute(up, "s", ring)
    high = lax.ppermute(down, "s", [(j, i) for i, j in ring])
    twin = [(i, i ^ 1) for i in range(lax.axis_size("gy"))]
    far = lax.ppermute(got[:, PAIR * BX :], "gy", twin)
    far_low = lax.ppermute(low[PAIR * DEEP :], "gy", twin)
    far_high = lax.ppermute(high[PAIR * DEEP :], "gy", twin)
    filtered = call(
        filter_kernel,
        f32(group, PAIR, BX, BX, 128),
        [SMEM] + [VMEM] * 6,
        [
            pltpu.VMEM((PAIR, SLAB + 2 * DEEP, 48, 128), jnp.float32),
            pltpu.VMEM((PAIR, SLAB + 2 * FLAT, 48, 128), jnp.float32),
            pltpu.VMEM((PAIR, SLAB + FLAT, 48, 128), jnp.float32),
            pltpu.VMEM((SLAB + 2 * FLAT, 32, 128), jnp.float32),
        ],
    )(core.reshape(1), got, low, high, far, far_low, far_high)
    back = lax.all_to_all(filtered, ("z", "gy"), 0, 0, tiled=True).reshape(n, BX, BX, 128)
    devices = slabs * group
    cells = float(devices * BX * BX * 128)
    parts = call(
        functools.partial(gram_kernel, 1.0 / cells), f32(devices, 8, 128), [VMEM]
    )(back)
    parts = lax.all_to_all(parts, ("s", "z", "gy"), 0, 0, tiled=True)
    return call(finish_kernel, (f32(n, BX, BX, 128), f32(n, n)), [VMEM, VMEM])(parts, back)


def solution(mesh):
    shape = mesh.devices.shape
    fine = Mesh(mesh.devices.reshape(shape[0] // 4, 4, shape[1]), ("s", "z", "gy"))
    return jax.shard_map(
        per_device,
        mesh=fine,
        in_specs=(P(None, ("s", "z"), "gy", None), P(("s", "z"), "gy", None)),
        out_specs=(P(None, ("s", "z"), "gy", None), P()),
        check_vma=False,
    )
```

```python
import functools

import jax
import jax.numpy as jnp
from jax import lax
from jax.experimental import pallas as pl
from jax.experimental.pallas import tpu as pltpu
from jax.sharding import Mesh
from jax.sharding import PartitionSpec as P

stencil_weights = (
    -5369.0 / 1800.0,
    12.0 / 7.0,
    -15.0 / 56.0,
    10.0 / 189.0,
    -1.0 / 112.0,
    2.0 / 1925.0,
    -1.0 / 16632.0,
)
grid_spacing = 0.5
filter_low = 4.0
filter_high = 46.0
centre_shift = 0.5 * (filter_high + filter_low)
half_width = 0.5 * (filter_high - filter_low)
kinetic = -0.5 / grid_spacing**2
diagonal = (kinetic * 3.0 * stencil_weights[0] - centre_shift) / half_width
coupling = tuple(kinetic * w / half_width for w in stencil_weights)
highest = lax.Precision.HIGHEST

REACH = 6
DEEP = 3 * REACH
FLAT = 2 * REACH
PAIR = 2
BX = 8
BLOCK = BX + 2
SLAB = 4 * BX
VMEM = pl.BlockSpec(memory_space=pltpu.VMEM)
SMEM = pl.BlockSpec(memory_space=pltpu.SMEM)


def gather(got, z, xi, yi):
    return got[pl.ds(((z * 4) * PAIR * BLOCK + xi) * BX + yi, 8, stride=BLOCK * BX), :]


def pack_kernel(got, up, down, up_pot, down_pot, mid_pot):
    for dest, first in ((up, SLAB - DEEP), (down, 0)):
        for i in range(DEEP):
            z, xi = divmod(first + i, BX)
            for yi in range(BX):
                dest[i, yi] = gather(got, z, xi, yi)
    for z in range(4):
        for k in range(2):
            for yi in range(BX):
                tile = gather(got, z, BX + k, yi)
                mid_pot[2 * z + k, yi] = tile
                if z >= 2:
                    up_pot[2 * z - 4 + k, yi] = tile
                else:
                    down_pot[2 * z + k, yi] = tile


def put(field, row, tiles):
    for yi in range(BX):
        field[row, REACH + yi] = tiles[yi]
        if yi >= BX - REACH:
            field[row, REACH + yi - BX] = pltpu.roll(tiles[yi], PAIR, 0)
        if yi < REACH:
            field[row, REACH + yi + BX] = pltpu.roll(tiles[yi], 8 - PAIR, 0)


def filter_kernel(
    core, got, low, high, low_pot, high_pot, mid_pot, far_low, far_high, far_mid,
    out, field0, field1, field2, pot,
):
    mine = core[0]

    def edge(i, carry):
        put(field0, i, [low[i, yi] for yi in range(BX)])
        put(field0, DEEP + SLAB + i, [high[i, yi] for yi in range(BX)])
        return carry

    lax.fori_loop(0, DEEP, edge, 0)
    for z in range(4):
        def inner(xi, carry, z=z):
            put(field0, DEEP + z * BX + xi, [gather(got, z, xi, yi) for yi in range(BX)])
            return carry

        lax.fori_loop(0, BX, inner, 0)

    odd = iota((8, 128), 0) % 2 == 1

    def put_pot(row, source, i, yi, parity, skip):
        tile = diagonal + source[i, yi] * (1.0 / half_width)
        if skip != 0:
            pot[row + parity, yi] = jnp.where(odd, pltpu.roll(tile, 1, 0), tile)
        if skip != 1:
            pot[row + 4 + parity, yi] = jnp.where(odd, tile, pltpu.roll(tile, 7, 0))

    for sources, row, count, skip in (
        ((low_pot, far_low), FLAT - 2 * BX, 2, (0, None)),
        ((mid_pot, far_mid), FLAT, 4, (None,) * 4),
        ((high_pot, far_high), FLAT + SLAB, 2, (None, 1)),
    ):
        for z in range(count):
            for k in range(2):
                for source, parity in zip(sources, (mine, 1 - mine)):
                    for yi in range(BX):
                        put_pot(
                            row + z * BX + 2 * k, source, 2 * z + k, yi, parity, skip[z]
                        )

    def apply(field, row, pot_row):
        line = [field[row, e] for e in range(BX + 2 * REACH)]
        totals = []
        for yi in range(BX):
            e = REACH + yi
            v = line[e]
            total = pot[pot_row, yi] * v
            for j in range(1, REACH + 1):
                near = (field[row + j, e] + field[row - j, e]) + (line[e + j] + line[e - j])
                near = near + (pltpu.roll(v, j, 1) + pltpu.roll(v, 128 - j, 1))
                total = total + coupling[j] * near
            totals.append(total)
        return totals

    def first(i, carry):
        put(field1, i, apply(field0, i + REACH, i))
        return carry

    lax.fori_loop(0, SLAB + 2 * FLAT, first, 0)

    def second(i, carry):
        ts = apply(field1, i + REACH, i + REACH)
        put(field2, i, [t + t - field0[i + FLAT, REACH + yi] for yi, t in enumerate(ts)])
        return carry

    lax.fori_loop(0, SLAB + FLAT, second, 0)

    for z in range(4):
        def third(xi, carry, z=z):
            i = z * BX + xi
            for yi, t in enumerate(apply(field2, i + REACH, i + FLAT)):
                start = (z * 4 * PAIR * BX + xi) * BX + yi
                out[pl.ds(start, 8, stride=BX * BX), :] = t + t - field1[i + FLAT, REACH + yi]
            return carry

        lax.fori_loop(0, BX, third, 0)


def iota(shape, dim):
    return lax.broadcasted_iota(jnp.int32, shape, dim)


def spread(orbital_count):
    shape = (orbital_count * BX, orbital_count)
    return (iota(shape, 0) // BX == iota(shape, 1)).astype(jnp.float32)


def same_y(orbital_count):
    shape = (orbital_count * BX, orbital_count * BX)
    return iota(shape, 0) % BX == iota(shape, 1) % BX


def dot(a, b, dims=((1,), (0,))):
    return lax.dot_general(
        a, b, (dims, ((), ())), precision=highest, preferred_element_type=jnp.float32
    )


def gram_kernel(scale, y, out):
    n = y.shape[0]
    total = None
    for x in range(BX):
        block = y[:, x].reshape(n * BX, 128)
        part = dot(block, block, ((1,), (1,)))
        total = part if total is None else total + part
    total = jnp.where(same_y(n), total, 0.0) * scale
    ones = spread(n)
    gram = dot(dot(ones, total, ((0,), (0,))), ones)
    wide = jnp.concatenate([gram[8 * k : 8 * k + 8] for k in range(n // 8)], axis=1)
    for d in range(out.shape[0]):
        out[d] = wide


def finish_kernel(parts, y, out, factor):
    n = y.shape[0]
    wide = jnp.sum(parts[...], axis=0)
    gram = jnp.concatenate([wide[:, n * k : n * k + n] for k in range(n // 8)], axis=0)
    unit = (iota((n, n), 0) == iota((n, n), 1)).astype(jnp.float32)
    left = jnp.concatenate([gram, unit, jnp.zeros((n, 128 - 2 * n), jnp.float32)], axis=1)
    row_of = iota((n, 128), 0)
    done = jnp.zeros((n, 128), jnp.float32)
    for k in range(n):
        inverse = lax.rsqrt(left[k : k + 1, k : k + 1])
        row = left[k : k + 1] * inverse
        column = left[:, k : k + 1] * inverse
        done = jnp.where(row_of == k, row, done)
        left = left - jnp.where(row_of > k, column, 0.0) * row
    factor[...] = jnp.where(iota((n, n), 0) <= iota((n, n), 1), done[:, :n], 0.0)
    mixer = done[:, n : 2 * n]
    ones = spread(n)
    wide_mixer = jnp.where(same_y(n), dot(dot(ones, mixer), ones, ((1,), (1,))), 0.0)
    for x in range(BX):
        block = y[:, x].reshape(n * BX, 128)
        out[:, x] = dot(wide_mixer, block).reshape(n, BX, 128)


def call(kernel, out_shape, in_specs, scratch=(), flops=0, moved=0):
    return pl.pallas_call(
        kernel,
        out_shape=out_shape,
        in_specs=in_specs,
        out_specs=jax.tree.map(lambda _: VMEM, out_shape),
        scratch_shapes=list(scratch),
        cost_estimate=pl.CostEstimate(flops=flops, bytes_accessed=moved, transcendentals=0),
    )


def f32(*shape):
    return jax.ShapeDtypeStruct(shape, jnp.float32)


def per_device(orbitals, potential):
    n = orbitals.shape[0]
    slabs = lax.axis_size("s")
    group = lax.axis_size("z") * lax.axis_size("gy")
    core = lax.axis_index("gy") % 2
    halves = potential.reshape(2, 2, 2, BX, 128).transpose(2, 0, 1, 3, 4)
    halves = jnp.broadcast_to(halves[None], (group // 2, 2, PAIR, 2, BX, 128))
    sent = jnp.concatenate(
        [orbitals.reshape(group, PAIR, BX, BX, 128), halves.reshape(group, PAIR, 2, BX, 128)],
        axis=2,
    )
    got = lax.all_to_all(sent, ("z", "gy"), 0, 0, tiled=True)
    got = got.reshape(group * PAIR * BLOCK * BX, 128)
    up, down, up_pot, down_pot, mid_pot = call(
        pack_kernel, (f32(DEEP, 8, 8, 128),) * 2 + (f32(4, 8, 8, 128),) * 2 + (f32(8, 8, 8, 128),), [VMEM]
    )(got)
    ring = [(i, (i + 1) % slabs) for i in range(slabs)]
    back_ring = [(j, i) for i, j in ring]
    twin = [(i, i ^ 1) for i in range(lax.axis_size("gy"))]
    low_pot = lax.ppermute(up_pot, "s", ring)
    high_pot = lax.ppermute(down_pot, "s", back_ring)
    low = lax.ppermute(up, "s", ring)
    high = lax.ppermute(down, "s", back_ring)
    far_mid = lax.ppermute(mid_pot, "gy", twin)
    far_low = lax.ppermute(low_pot, "gy", twin)
    far_high = lax.ppermute(high_pot, "gy", twin)
    wide = BX + 2 * REACH
    filtered = call(
        filter_kernel,
        f32(group * PAIR * BX * BX, 128),
        [SMEM] + [VMEM] * 9,
        [
            pltpu.VMEM((SLAB + 2 * DEEP, wide, 8, 128), jnp.float32),
            pltpu.VMEM((SLAB + 2 * FLAT, wide, 8, 128), jnp.float32),
            pltpu.VMEM((SLAB + FLAT, wide, 8, 128), jnp.float32),
            pltpu.VMEM((SLAB + 2 * FLAT, BX, 8, 128), jnp.float32),
        ],
    )(core.reshape(1), got, low, high, low_pot, high_pot, mid_pot, far_low, far_high, far_mid)
    filtered = filtered.reshape(group, PAIR, BX, BX, 128)
    back = lax.all_to_all(filtered, ("z", "gy"), 0, 0, tiled=True).reshape(n, BX, BX, 128)
    devices = slabs * group
    cells = float(devices * BX * BX * 128)
    parts = call(
        functools.partial(gram_kernel, 1.0 / cells), f32(devices, 8, 128), [VMEM]
    )(back)
    parts = lax.all_to_all(parts, ("s", "z", "gy"), 0, 0, tiled=True)
    return call(finish_kernel, (f32(n, BX, BX, 128), f32(n, n)), [VMEM, VMEM])(parts, back)


def solution(mesh):
    shape = mesh.devices.shape
    fine = Mesh(mesh.devices.reshape(shape[0] // 4, 4, shape[1]), ("s", "z", "gy"))
    return jax.shard_map(
        per_device,
        mesh=fine,
        in_specs=(P(None, ("s", "z"), "gy", None), P(("s", "z"), "gy", None)),
        out_specs=(P(None, ("s", "z"), "gy", None), P()),
        check_vma=False,
    )
```

```python
import functools

import jax
import jax.numpy as jnp
from jax import lax
from jax.experimental import pallas as pl
from jax.experimental.pallas import tpu as pltpu
from jax.sharding import Mesh
from jax.sharding import PartitionSpec as P

stencil_weights = (
    -5369.0 / 1800.0,
    12.0 / 7.0,
    -15.0 / 56.0,
    10.0 / 189.0,
    -1.0 / 112.0,
    2.0 / 1925.0,
    -1.0 / 16632.0,
)
grid_spacing = 0.5
filter_low = 4.0
filter_high = 46.0
centre_shift = 0.5 * (filter_high + filter_low)
half_width = 0.5 * (filter_high - filter_low)
kinetic = -0.5 / grid_spacing**2
diagonal = (kinetic * 3.0 * stencil_weights[0] - centre_shift) / half_width
coupling = tuple(kinetic * w / half_width for w in stencil_weights)
highest = lax.Precision.HIGHEST

REACH = 6
DEEP = 3 * REACH
FLAT = 2 * REACH
PAIR = 2
BX = 8
BLOCK = BX + 2
CHUNK = 4
SLAB = 4 * BX
VMEM = pl.BlockSpec(memory_space=pltpu.VMEM)
SMEM = pl.BlockSpec(memory_space=pltpu.SMEM)


def gather(got, z, xi, yi):
    return got[pl.ds(((z * 4) * PAIR * BLOCK + xi) * BX + yi, 8, stride=BLOCK * BX), :]


def pack_kernel(got, up, down, up_pot, down_pot, mid_pot):
    for dest, first in ((up, SLAB - DEEP), (down, 0)):
        for i in range(DEEP):
            z, xi = divmod(first + i, BX)
            for yi in range(BX):
                dest[i, yi] = gather(got, z, xi, yi)
    for z in range(4):
        for k in range(2):
            for yi in range(BX):
                tile = gather(got, z, BX + k, yi)
                mid_pot[2 * z + k, yi] = tile
                if z >= 2:
                    up_pot[2 * z - 4 + k, yi] = tile
                else:
                    down_pot[2 * z + k, yi] = tile


def put(field, row, tiles):
    for yi in range(BX):
        field[row, REACH + yi] = tiles[yi]
        if yi >= BX - REACH:
            field[row, REACH + yi - BX] = pltpu.roll(tiles[yi], PAIR, 0)
        if yi < REACH:
            field[row, REACH + yi + BX] = pltpu.roll(tiles[yi], 8 - PAIR, 0)


def parts_of(v):
    high = v.astype(jnp.bfloat16)
    rest = v - high.astype(jnp.float32)
    middle = rest.astype(jnp.bfloat16)
    return high, middle, (rest - middle.astype(jnp.float32)).astype(jnp.bfloat16)


def band_parts():
    apart = (iota((128, 128), 0) - iota((128, 128), 1)) % 128
    band = jnp.zeros((128, 128), jnp.float32)
    for j in range(1, REACH + 1):
        band = jnp.where((apart == j) | (apart == 128 - j), coupling[j], band)
    high, middle, low = parts_of(band)
    top = jnp.concatenate([high, middle], axis=1)
    return jnp.concatenate([top, top], axis=0)


def band_product(v, bands):
    high, middle, _ = parts_of(v)
    both = jnp.dot(
        jnp.concatenate([high, middle], axis=1), bands, preferred_element_type=jnp.float32
    )
    return both[:, :128] + both[:, 128:]


def filter_kernel(
    core, got, low, high, low_pot, high_pot, mid_pot, far_low, far_high, far_mid,
    out, field0, field1, field2, pot, far_z,
):
    mine = core[0]
    bands = band_parts()

    def edge(i, carry):
        put(field0, i, [low[i, yi] for yi in range(BX)])
        put(field0, DEEP + SLAB + i, [high[i, yi] for yi in range(BX)])
        return carry

    lax.fori_loop(0, DEEP, edge, 0)
    for z in range(4):
        def inner(xi, carry, z=z):
            put(field0, DEEP + z * BX + xi, [gather(got, z, xi, yi) for yi in range(BX)])
            return carry

        lax.fori_loop(0, BX, inner, 0)

    odd = iota((8, 128), 0) % 2 == 1

    def put_pot(row, source, i, yi, parity, skip):
        tile = diagonal + source[i, yi] * (1.0 / half_width)
        if skip != 0:
            pot[row + parity, yi] = jnp.where(odd, pltpu.roll(tile, 1, 0), tile)
        if skip != 1:
            pot[row + 4 + parity, yi] = jnp.where(odd, tile, pltpu.roll(tile, 7, 0))

    for sources, row, count, skip in (
        ((low_pot, far_low), FLAT - 2 * BX, 2, (0, None)),
        ((mid_pot, far_mid), FLAT, 4, (None,) * 4),
        ((high_pot, far_high), FLAT + SLAB, 2, (None, 1)),
    ):
        for z in range(count):
            for k in range(2):
                for source, parity in zip(sources, (mine, 1 - mine)):
                    for yi in range(BX):
                        put_pot(
                            row + z * BX + 2 * k, source, 2 * z + k, yi, parity, skip[z]
                        )

    def along_z(field, start, i):
        v = field[pl.ds(start, CHUNK), REACH : REACH + BX].reshape(CHUNK * BX * 8, 128)
        far_z[pl.ds(i, CHUNK)] = band_product(v, bands).reshape(CHUNK, BX, 8, 128)

    def sweep(field, rows, one):
        along_z(field, REACH, 0)

        def chunk(c, carry):
            for r in range(0, CHUNK, 2):
                one(c * CHUNK + r)
            ahead = (c + 1) * CHUNK
            along_z(field, REACH + ahead, ahead)
            return carry

        lax.fori_loop(0, rows // CHUNK, chunk, 0)

    def apply(field, row, pot_row, i):
        totals = [[], []]
        for begin in range(0, BX, 4):
            lines = [
                [field[row + r, e] for e in range(begin, begin + 4 + 2 * REACH)] for r in range(2)
            ]
            for yi in range(begin, begin + 4):
                e = REACH + yi - begin
                x = {0: lines[0][e], 1: lines[1][e]}
                for d in (*range(-REACH, 0), *range(2, REACH + 2)):
                    x[d] = field[row + d, REACH + yi]
                for r in range(2):
                    line = lines[r]
                    total = pot[pot_row + r, yi] * line[e] + far_z[i + r, yi]
                    for j in range(1, REACH + 1):
                        near = (x[r + j] + x[r - j]) + (line[e + j] + line[e - j])
                        total = total + coupling[j] * near
                    totals[r].append(total)
        return totals

    def first(i):
        for r, ts in enumerate(apply(field0, i + REACH, i, i)):
            put(field1, i + r, ts)

    def second(i):
        for r, ts in enumerate(apply(field1, i + REACH, i + REACH, i)):
            before = i + r + FLAT
            put(field2, i + r, [t + t - field0[before, REACH + yi] for yi, t in enumerate(ts)])

    def third(i):
        for r, ts in enumerate(apply(field2, i + REACH, i + FLAT, i)):
            for yi, t in enumerate(ts):
                start = ((i // BX) * 4 * PAIR * BX + i % BX + r) * BX + yi
                out[pl.ds(start, 8, stride=BX * BX), :] = (
                    t + t - field1[i + r + FLAT, REACH + yi]
                )

    sweep(field0, SLAB + 2 * FLAT, first)
    sweep(field1, SLAB + FLAT, second)
    sweep(field2, SLAB, third)


def iota(shape, dim):
    return lax.broadcasted_iota(jnp.int32, shape, dim)


def spread(orbital_count):
    shape = (orbital_count * BX, orbital_count)
    return (iota(shape, 0) // BX == iota(shape, 1)).astype(jnp.float32)


def same_y(orbital_count):
    shape = (orbital_count * BX, orbital_count * BX)
    return iota(shape, 0) % BX == iota(shape, 1) % BX


def dot(a, b, dims=((1,), (0,))):
    return lax.dot_general(
        a, b, (dims, ((), ())), precision=highest, preferred_element_type=jnp.float32
    )


def pair_of_rows(y, x):
    rows = y.shape[0] * BX
    return jnp.concatenate([y[:, x].reshape(rows, 128), y[:, x + 1].reshape(rows, 128)], axis=1)


def gram_kernel(scale, y, out):
    n = y.shape[0]
    total = None
    for x in range(0, BX, 2):
        block = pair_of_rows(y, x)
        part = dot(block, block, ((1,), (1,)))
        total = part if total is None else total + part
    total = jnp.where(same_y(n), total, 0.0) * scale
    ones = spread(n)
    gram = dot(dot(ones, total, ((0,), (0,))), ones)
    wide = jnp.concatenate([gram[8 * k : 8 * k + 8] for k in range(n // 8)], axis=1)
    for d in range(out.shape[0]):
        out[d] = wide


def finish_kernel(parts, y, out, factor):
    n = y.shape[0]
    wide = jnp.sum(parts[...], axis=0)
    gram = jnp.concatenate([wide[:, n * k : n * k + n] for k in range(n // 8)], axis=0)
    unit = (iota((n, n), 0) == iota((n, n), 1)).astype(jnp.float32)
    left = jnp.concatenate([gram, unit, jnp.zeros((n, 128 - 2 * n), jnp.float32)], axis=1)
    row_of = iota((n, 128), 0)
    done = jnp.zeros((n, 128), jnp.float32)
    for k in range(n):
        inverse = lax.rsqrt(left[k : k + 1, k : k + 1])
        row = left[k : k + 1] * inverse
        column = left[:, k : k + 1] * inverse
        done = jnp.where(row_of == k, row, done)
        left = left - jnp.where(row_of > k, column, 0.0) * row
    factor[...] = jnp.where(iota((n, n), 0) <= iota((n, n), 1), done[:, :n], 0.0)
    mixer = done[:, n : 2 * n]
    ones = spread(n)
    wide_mixer = jnp.where(same_y(n), dot(dot(ones, mixer), ones, ((1,), (1,))), 0.0)
    for x in range(0, BX, 2):
        mixed = dot(wide_mixer, pair_of_rows(y, x))
        out[:, x] = mixed[:, :128].reshape(n, BX, 128)
        out[:, x + 1] = mixed[:, 128:].reshape(n, BX, 128)


def call(kernel, out_shape, in_specs, scratch=(), limit=8, flops=0, moved=0):
    return pl.pallas_call(
        kernel,
        out_shape=out_shape,
        in_specs=in_specs,
        out_specs=jax.tree.map(lambda _: VMEM, out_shape),
        scratch_shapes=list(scratch),
        compiler_params=pltpu.CompilerParams(vmem_limit_bytes=limit << 20),
        cost_estimate=pl.CostEstimate(flops=flops, bytes_accessed=moved, transcendentals=0),
    )


def f32(*shape):
    return jax.ShapeDtypeStruct(shape, jnp.float32)


def per_device(orbitals, potential):
    n = orbitals.shape[0]
    slabs = lax.axis_size("s")
    group = lax.axis_size("z") * lax.axis_size("gy")
    core = lax.axis_index("gy") % 2
    halves = potential.reshape(2, 2, 2, BX, 128).transpose(2, 0, 1, 3, 4)
    halves = jnp.broadcast_to(halves[None], (group // 2, 2, PAIR, 2, BX, 128))
    sent = jnp.concatenate(
        [orbitals.reshape(group, PAIR, BX, BX, 128), halves.reshape(group, PAIR, 2, BX, 128)],
        axis=2,
    )
    got = lax.all_to_all(sent, ("z", "gy"), 0, 0, tiled=True)
    got = got.reshape(group * PAIR * BLOCK * BX, 128)
    up, down, up_pot, down_pot, mid_pot = call(
        pack_kernel, (f32(DEEP, 8, 8, 128),) * 2 + (f32(4, 8, 8, 128),) * 2 + (f32(8, 8, 8, 128),), [VMEM]
    )(got)
    ring = [(i, (i + 1) % slabs) for i in range(slabs)]
    back_ring = [(j, i) for i, j in ring]
    twin = [(i, i ^ 1) for i in range(lax.axis_size("gy"))]
    low_pot = lax.ppermute(up_pot, "s", ring)
    high_pot = lax.ppermute(down_pot, "s", back_ring)
    low = lax.ppermute(up, "s", ring)
    high = lax.ppermute(down, "s", back_ring)
    far_mid = lax.ppermute(mid_pot, "gy", twin)
    far_low = lax.ppermute(low_pot, "gy", twin)
    far_high = lax.ppermute(high_pot, "gy", twin)
    wide = BX + 2 * REACH
    filtered = call(
        filter_kernel,
        f32(group * PAIR * BX * BX, 128),
        [SMEM] + [VMEM] * 9,
        [
            pltpu.VMEM((SLAB + 2 * DEEP, wide, 8, 128), jnp.float32),
            pltpu.VMEM((SLAB + 2 * FLAT, wide, 8, 128), jnp.float32),
            pltpu.VMEM((SLAB + FLAT, wide, 8, 128), jnp.float32),
            pltpu.VMEM((SLAB + 2 * FLAT, BX, 8, 128), jnp.float32),
            pltpu.VMEM((SLAB + 2 * FLAT + CHUNK, BX, 8, 128), jnp.float32),
        ],
        32,
    )(core.reshape(1), got, low, high, low_pot, high_pot, mid_pot, far_low, far_high, far_mid)
    filtered = filtered.reshape(group, PAIR, BX, BX, 128)
    back = lax.all_to_all(filtered, ("z", "gy"), 0, 0, tiled=True).reshape(n, BX, BX, 128)
    devices = slabs * group
    cells = float(devices * BX * BX * 128)
    parts = call(
        functools.partial(gram_kernel, 1.0 / cells), f32(devices, 8, 128), [VMEM]
    )(back)
    parts = lax.all_to_all(parts, ("s", "z", "gy"), 0, 0, tiled=True)
    return call(finish_kernel, (f32(n, BX, BX, 128), f32(n, n)), [VMEM, VMEM])(parts, back)


def solution(mesh):
    shape = mesh.devices.shape
    fine = Mesh(mesh.devices.reshape(shape[0] // 4, 4, shape[1]), ("s", "z", "gy"))
    return jax.shard_map(
        per_device,
        mesh=fine,
        in_specs=(P(None, ("s", "z"), "gy", None), P(("s", "z"), "gy", None)),
        out_specs=(P(None, ("s", "z"), "gy", None), P()),
        check_vma=False,
    )
```

```python
import functools

import jax
import jax.numpy as jnp
from jax import lax
from jax.experimental import pallas as pl
from jax.experimental.pallas import tpu as pltpu
from jax.sharding import Mesh
from jax.sharding import PartitionSpec as P

stencil_weights = (
    -5369.0 / 1800.0,
    12.0 / 7.0,
    -15.0 / 56.0,
    10.0 / 189.0,
    -1.0 / 112.0,
    2.0 / 1925.0,
    -1.0 / 16632.0,
)
grid_spacing = 0.5
filter_low = 4.0
filter_high = 46.0
centre_shift = 0.5 * (filter_high + filter_low)
half_width = 0.5 * (filter_high - filter_low)
kinetic = -0.5 / grid_spacing**2
diagonal = (kinetic * 3.0 * stencil_weights[0] - centre_shift) / half_width
coupling = tuple(kinetic * w / half_width for w in stencil_weights)
highest = lax.Precision.HIGHEST

REACH = 6
DEEP = 3 * REACH
FLAT = 2 * REACH
STEP = 4
PAIR = 2
BX = 8
BLOCK = BX + 2
SLAB = 4 * BX
VMEM = pl.BlockSpec(memory_space=pltpu.VMEM)
SMEM = pl.BlockSpec(memory_space=pltpu.SMEM)


def gather(got, z, xi, yi):
    return got[pl.ds(((z * 4) * PAIR * BLOCK + xi) * BX + yi, 8, stride=BLOCK * BX), :]


def pack_kernel(got, up, down, up_pot, down_pot, mid_pot):
    for dest, first in ((up, SLAB - DEEP), (down, 0)):
        for i in range(DEEP):
            z, xi = divmod(first + i, BX)
            for yi in range(BX):
                dest[i, yi] = gather(got, z, xi, yi)
    for z in range(4):
        for k in range(2):
            for yi in range(BX):
                tile = gather(got, z, BX + k, yi)
                mid_pot[2 * z + k, yi] = tile
                if z >= 2:
                    up_pot[2 * z - 4 + k, yi] = tile
                else:
                    down_pot[2 * z + k, yi] = tile


def put(field, row, tiles):
    for yi in range(BX):
        field[row, yi, 0:8] = tiles[yi]
        field[row, yi, 8:16] = tiles[yi]


def take(field, row, yi):
    first = 8 - PAIR if yi < 0 else PAIR if yi >= BX else 0
    return field[row, yi % BX, first : first + 8]


def parts_of(v):
    high = v.astype(jnp.bfloat16)
    rest = v - high.astype(jnp.float32)
    middle = rest.astype(jnp.bfloat16)
    return high, middle, (rest - middle.astype(jnp.float32)).astype(jnp.bfloat16)


def band_parts():
    apart = (iota((128, 128), 0) - iota((128, 128), 1)) % 128
    band = jnp.zeros((128, 128), jnp.float32)
    for j in range(1, REACH + 1):
        band = jnp.where((apart == j) | (apart == 128 - j), coupling[j], band)
    high, middle, low = parts_of(band)
    top = jnp.concatenate([high, middle], axis=1)
    return jnp.concatenate([top, top], axis=0)


def band_product(v, bands):
    high, middle, _ = parts_of(v)
    both = jnp.dot(
        jnp.concatenate([high, middle], axis=1), bands, preferred_element_type=jnp.float32
    )
    return both[:, :128] + both[:, 128:]


def filter_kernel(
    core, got, low, high, low_pot, high_pot, mid_pot, far_low, far_high, far_mid,
    out, field0, field1, field2, pot, far_z,
):
    mine = core[0]
    bands = band_parts()

    def edge(i, carry):
        put(field0, i, [low[i, yi] for yi in range(BX)])
        put(field0, DEEP + SLAB + i, [high[i, yi] for yi in range(BX)])
        return carry

    lax.fori_loop(0, DEEP, edge, 0)
    for z in range(4):
        def inner(xi, carry, z=z):
            put(field0, DEEP + z * BX + xi, [gather(got, z, xi, yi) for yi in range(BX)])
            return carry

        lax.fori_loop(0, BX, inner, 0)

    odd = iota((8, 128), 0) % 2 == 1

    def put_pot(row, source, i, yi, parity, skip):
        tile = diagonal + source[i, yi] * (1.0 / half_width)
        if skip != 0:
            pot[row + parity, yi] = jnp.where(odd, pltpu.roll(tile, 1, 0), tile)
        if skip != 1:
            pot[row + 4 + parity, yi] = jnp.where(odd, tile, pltpu.roll(tile, 7, 0))

    for sources, row, count, skip in (
        ((low_pot, far_low), FLAT - 2 * BX, 2, (0, None)),
        ((mid_pot, far_mid), FLAT, 4, (None,) * 4),
        ((high_pot, far_high), FLAT + SLAB, 2, (None, 1)),
    ):
        for z in range(count):
            for k in range(2):
                for source, parity in zip(sources, (mine, 1 - mine)):
                    for yi in range(BX):
                        put_pot(
                            row + z * BX + 2 * k, source, 2 * z + k, yi, parity, skip[z]
                        )

    def along_z(field, start, i, count):
        v = field[pl.ds(start, count), :, 0:8].reshape(count * BX * 8, 128)
        far_z[pl.ds(i, count)] = band_product(v, bands).reshape(count, BX, 8, 128)

    def sweep(field, rows, count, one):
        along_z(field, REACH, 0, count)

        def chunk(c, carry):
            for r in range(0, count, 2):
                one(c * count + r)
            ahead = (c + 1) * count
            along_z(field, REACH + ahead, ahead, count)
            return carry

        lax.fori_loop(0, rows // count - 1, chunk, 0)
        for r in range(rows - count, rows, 2):
            one(r)

    def apply(field, row, pot_row, i):
        totals = [[], []]
        for begin in range(0, BX, 4):
            lines = [
                [take(field, row + r, y) for y in range(begin - REACH, begin + 4 + REACH)]
                for r in range(2)
            ]
            for yi in range(begin, begin + 4):
                e = REACH + yi - begin
                x = {0: lines[0][e], 1: lines[1][e]}
                for d in (*range(-REACH, 0), *range(2, REACH + 2)):
                    x[d] = take(field, row + d, yi)
                for r in range(2):
                    line = lines[r]
                    total = pot[pot_row + r, yi] * line[e] + far_z[i + r, yi]
                    for j in range(1, REACH + 1):
                        near = (x[r + j] + x[r - j]) + (line[e + j] + line[e - j])
                        total = total + coupling[j] * near
                    totals[r].append(total)
        return totals

    def first(i):
        for r, ts in enumerate(apply(field0, i + REACH, i, i)):
            put(field1, i + r, ts)

    def second(i):
        for r, ts in enumerate(apply(field1, i + REACH, i + REACH, i)):
            before = i + r + FLAT
            put(field2, i + r, [t + t - take(field0, before, yi) for yi, t in enumerate(ts)])

    def third(i):
        for r, ts in enumerate(apply(field2, i + REACH, i + FLAT, i)):
            for yi, t in enumerate(ts):
                start = ((i // BX) * 4 * PAIR * BX + i % BX + r) * BX + yi
                out[pl.ds(start, 8, stride=BX * BX), :] = (
                    t + t - take(field1, i + r + FLAT, yi)
                )

    sweep(field0, SLAB + 2 * FLAT, 14, first)
    sweep(field1, SLAB + FLAT, 22, second)
    sweep(field2, SLAB, 16, third)


def iota(shape, dim):
    return lax.broadcasted_iota(jnp.int32, shape, dim)


def spread(orbital_count):
    shape = (orbital_count * BX, orbital_count)
    return (iota(shape, 0) // BX == iota(shape, 1)).astype(jnp.float32)


def same_y(orbital_count):
    shape = (orbital_count * BX, orbital_count * BX)
    return iota(shape, 0) % BX == iota(shape, 1) % BX


def dot(a, b, dims=((1,), (0,))):
    return lax.dot_general(
        a, b, (dims, ((), ())), precision=highest, preferred_element_type=jnp.float32
    )


def pair_of_rows(y, x):
    rows = y.shape[0] * BX
    return jnp.concatenate([y[:, x].reshape(rows, 128), y[:, x + 1].reshape(rows, 128)], axis=1)


def gram_kernel(scale, y, out):
    n = y.shape[0]
    total = None
    for x in range(0, BX, 2):
        block = pair_of_rows(y, x)
        part = dot(block, block, ((1,), (1,)))
        total = part if total is None else total + part
    total = jnp.where(same_y(n), total, 0.0) * scale
    ones = spread(n)
    gram = dot(dot(ones, total, ((0,), (0,))), ones)
    half = n // 2
    upper = iota((half, half), 0) <= iota((half, half), 1)
    kept = jnp.concatenate(
        [jnp.where(upper, gram[:half, :half], gram[half:, half:]), gram[:half, half:]], axis=1
    )
    unit = iota((half, half), 0) == iota((half, half), 1)
    ends = jnp.sum(jnp.where(unit, gram[half:, half:], 0.0), axis=0, keepdims=True)
    ends = jnp.concatenate([ends, jnp.zeros((1, 128 - half), jnp.float32)], axis=1)
    rows = jnp.concatenate([kept[4 * k : 4 * k + 4] for k in range(4)], axis=1)
    rows = jnp.concatenate([rows, ends], axis=0)
    for d in range(out.shape[0] // 5):
        out[5 * d : 5 * d + 5] = rows


def finish_kernel(parts, y, out, factor):
    n = y.shape[0]
    half = n // 2
    rows = []
    for r in range(5):
        total = None
        for d in range(0, parts.shape[0] // 5, 8):
            tile = parts[pl.ds(5 * d + r, 8, stride=5), :]
            total = tile if total is None else total + tile
        rows.append(jnp.sum(total, axis=0, keepdims=True))
    rows = jnp.concatenate(rows, axis=0)
    kept = jnp.concatenate([rows[:4, n * k : n * k + n] for k in range(4)], axis=0)
    across = kept[:, half:]
    unit = iota((half, half), 0) == iota((half, half), 1)
    upper = iota((half, half), 0) < iota((half, half), 1)
    mixed = kept[:, :half]
    turned = mixed.T
    first = jnp.where(upper | unit, mixed, turned)
    last = jnp.where(upper, turned, mixed)
    last = jnp.where(unit, jnp.broadcast_to(rows[4:5, :half], (half, half)), last)
    gram = jnp.concatenate(
        [jnp.concatenate([first, across], axis=1), jnp.concatenate([across.T, last], axis=1)],
        axis=0,
    )
    unit = (iota((n, n), 0) == iota((n, n), 1)).astype(jnp.float32)
    left = jnp.concatenate([gram, unit, jnp.zeros((n, 128 - 2 * n), jnp.float32)], axis=1)
    row_of = iota((n, 128), 0)
    finished = []
    for k in range(0, n, STEP):
        entry = {
            (i, j): jnp.broadcast_to(left[k + i : k + i + 1, k + j : k + j + 1], (1, 128))
            for i in range(STEP)
            for j in range(i + 1)
        }
        columns = [
            jnp.broadcast_to(left[:, k + j : k + j + 1], (n, 128)) for j in range(STEP)
        ]
        lines = [left[k + j : k + j + 1] for j in range(STEP)]
        for j in range(STEP):
            inverse = lax.rsqrt(entry[j, j])
            lines[j] = lines[j] * inverse
            columns[j] = columns[j] * inverse
            for i in range(j + 1, STEP):
                entry[i, j] = entry[i, j] * inverse
            for i in range(j + 1, STEP):
                for m in range(j + 1, i + 1):
                    entry[i, m] = entry[i, m] - entry[i, j] * entry[m, j]
                lines[i] = lines[i] - entry[i, j] * lines[j]
                columns[i] = columns[i] - entry[i, j] * columns[j]
        finished += lines
        change = None
        for line, column in zip(lines, columns):
            part = column * line
            change = part if change is None else change + part
        left = jnp.where(row_of >= k + STEP, left - change, left)
    done = jnp.concatenate(finished, axis=0)
    factor[...] = jnp.where(iota((n, n), 0) <= iota((n, n), 1), done[:, :n], 0.0)
    mixer = done[:, n : 2 * n]
    ones = spread(n)
    tall = jnp.broadcast_to(mixer[:, None], (n, BX, n)).reshape(n * BX, n)
    wide_mixer = jnp.where(same_y(n), dot(tall, ones, ((1,), (1,))), 0.0)
    for x in range(0, BX, 2):
        mixed = dot(wide_mixer, pair_of_rows(y, x))
        out[:, x] = mixed[:, :128].reshape(n, BX, 128)
        out[:, x + 1] = mixed[:, 128:].reshape(n, BX, 128)


def call(kernel, out_shape, in_specs, scratch=(), limit=8, flops=0, moved=0):
    return pl.pallas_call(
        kernel,
        out_shape=out_shape,
        in_specs=in_specs,
        out_specs=jax.tree.map(lambda _: VMEM, out_shape),
        scratch_shapes=list(scratch),
        compiler_params=pltpu.CompilerParams(vmem_limit_bytes=limit << 20),
        cost_estimate=pl.CostEstimate(flops=flops, bytes_accessed=moved, transcendentals=0),
    )


def f32(*shape):
    return jax.ShapeDtypeStruct(shape, jnp.float32)


def per_device(orbitals, potential):
    n = orbitals.shape[0]
    slabs = lax.axis_size("s")
    group = lax.axis_size("z") * lax.axis_size("gy")
    core = lax.axis_index("gy") & 1
    halves = potential.reshape(2, 2, 2, BX, 128).transpose(2, 0, 1, 3, 4)
    halves = jnp.broadcast_to(halves[None], (group // 2, 2, PAIR, 2, BX, 128))
    sent = jnp.concatenate(
        [orbitals.reshape(group, PAIR, BX, BX, 128), halves.reshape(group, PAIR, 2, BX, 128)],
        axis=2,
    )
    got = lax.all_to_all(sent, ("z", "gy"), 0, 0, tiled=True)
    got = got.reshape(group * PAIR * BLOCK * BX, 128)
    up, down, up_pot, down_pot, mid_pot = call(
        pack_kernel, (f32(DEEP, 8, 8, 128),) * 2 + (f32(4, 8, 8, 128),) * 2 + (f32(8, 8, 8, 128),), [VMEM]
    )(got)
    ring = [(i, (i + 1) % slabs) for i in range(slabs)]
    back_ring = [(j, i) for i, j in ring]
    twin = [(i, i ^ 1) for i in range(lax.axis_size("gy"))]
    low_pot = lax.ppermute(up_pot, "s", ring)
    high_pot = lax.ppermute(down_pot, "s", back_ring)
    low = lax.ppermute(up, "s", ring)
    high = lax.ppermute(down, "s", back_ring)
    far_mid = lax.ppermute(mid_pot, "gy", twin)
    far_low = lax.ppermute(low_pot, "gy", twin)
    far_high = lax.ppermute(high_pot, "gy", twin)
    filtered = call(
        filter_kernel,
        f32(group * PAIR * BX * BX, 128),
        [SMEM] + [VMEM] * 9,
        [
            pltpu.VMEM((SLAB + 2 * DEEP, BX, 16, 128), jnp.float32),
            pltpu.VMEM((SLAB + 2 * FLAT, BX, 16, 128), jnp.float32),
            pltpu.VMEM((SLAB + FLAT, BX, 16, 128), jnp.float32),
            pltpu.VMEM((SLAB + 2 * FLAT, BX, 8, 128), jnp.float32),
            pltpu.VMEM((SLAB + 2 * FLAT, BX, 8, 128), jnp.float32),
        ],
        32,
    )(core.reshape(1), got, low, high, low_pot, high_pot, mid_pot, far_low, far_high, far_mid)
    filtered = filtered.reshape(group, PAIR, BX, BX, 128)
    back = lax.all_to_all(filtered, ("z", "gy"), 0, 0, tiled=True).reshape(n, BX, BX, 128)
    devices = slabs * group
    cells = float(devices * BX * BX * 128)
    parts = call(
        functools.partial(gram_kernel, 1.0 / cells), f32(devices * 5, 128), [VMEM]
    )(back)
    parts = lax.all_to_all(
        parts.reshape(devices, 1, 5 * 128), ("s", "z", "gy"), 0, 0, tiled=True
    ).reshape(devices * 5, 128)
    return call(finish_kernel, (f32(n, BX, BX, 128), f32(n, n)), [VMEM, VMEM])(parts, back)


def solution(mesh):
    shape = mesh.devices.shape
    fine = Mesh(mesh.devices.reshape(shape[0] // 4, 4, shape[1]), ("s", "z", "gy"))
    return jax.shard_map(
        per_device,
        mesh=fine,
        in_specs=(P(None, ("s", "z"), "gy", None), P(("s", "z"), "gy", None)),
        out_specs=(P(None, ("s", "z"), "gy", None), P()),
        check_vma=False,
    )
```

```python
import functools

import jax
import jax.numpy as jnp
from jax import lax
from jax.experimental import pallas as pl
from jax.experimental.pallas import tpu as pltpu
from jax.sharding import Mesh
from jax.sharding import PartitionSpec as P

stencil_weights = (
    -5369.0 / 1800.0,
    12.0 / 7.0,
    -15.0 / 56.0,
    10.0 / 189.0,
    -1.0 / 112.0,
    2.0 / 1925.0,
    -1.0 / 16632.0,
)
grid_spacing = 0.5
filter_low = 4.0
filter_high = 46.0
centre_shift = 0.5 * (filter_high + filter_low)
half_width = 0.5 * (filter_high - filter_low)
kinetic = -0.5 / grid_spacing**2
diagonal = (kinetic * 3.0 * stencil_weights[0] - centre_shift) / half_width
coupling = tuple(kinetic * w / half_width for w in stencil_weights)
highest = lax.Precision.HIGHEST

REACH = 6
DEEP = 3 * REACH
FLAT = 2 * REACH
STEP = 4
PAIR = 2
IN1 = (DEEP, DEEP + 20)
IN2 = (DEEP, DEEP + 8)
BX = 8
BLOCK = BX + 2
SLAB = 4 * BX
VMEM = pl.BlockSpec(memory_space=pltpu.VMEM)
SMEM = pl.BlockSpec(memory_space=pltpu.SMEM)


def gather(got, z, xi, yi):
    return got[pl.ds(((z * 4) * PAIR * BLOCK + xi) * BX + yi, 8, stride=BLOCK * BX), :]


def message_kernel(orbitals, potential, out):
    for d in range(out.shape[0]):
        for o in range(PAIR):
            for xi in range(BX):
                out[d, o, xi] = orbitals[d, o, xi]
            for k in range(2):
                out[d, o, BX + k] = potential[4 * o + 2 * k + d % 2]


def pack_kernel(got, up, down, up_pot, down_pot, mid_pot):
    for dest, first in ((up, SLAB - DEEP), (down, 0)):
        for i in range(DEEP):
            z, xi = divmod(first + i, BX)
            for yi in range(BX):
                dest[i, yi] = gather(got, z, xi, yi)
    for z in range(4):
        for k in range(2):
            for yi in range(BX):
                tile = gather(got, z, BX + k, yi)
                mid_pot[2 * z + k, yi] = tile
                if z >= 2:
                    up_pot[2 * z - 4 + k, yi] = tile
                else:
                    down_pot[2 * z + k, yi] = tile


def put(field, row, tiles):
    for yi in range(BX):
        field[row, yi, 0:8] = tiles[yi]
        field[row, yi, 8:16] = tiles[yi]


def take(field, row, yi):
    first = 8 - PAIR if yi < 0 else PAIR if yi >= BX else 0
    return field[row, yi % BX, first : first + 8]


def parts_of(v):
    high = v.astype(jnp.bfloat16)
    rest = v - high.astype(jnp.float32)
    middle = rest.astype(jnp.bfloat16)
    return high, middle, (rest - middle.astype(jnp.float32)).astype(jnp.bfloat16)


def band_parts():
    apart = (iota((128, 128), 0) - iota((128, 128), 1)) % 128
    band = jnp.zeros((128, 128), jnp.float32)
    for j in range(1, REACH + 1):
        band = jnp.where((apart == j) | (apart == 128 - j), coupling[j], band)
    high, middle, low = parts_of(band)
    top = jnp.concatenate([high, middle], axis=1)
    return jnp.concatenate([top, top], axis=0)


def band_product(v, bands):
    high, middle, _ = parts_of(v)
    both = jnp.dot(
        jnp.concatenate([high, middle], axis=1), bands, preferred_element_type=jnp.float32
    )
    return both[:, :128] + both[:, 128:]


def sweep(field, far_z, bands, first, last, count, one):
    def chunk(c, carry):
        start = first + c * count
        along_z(field, far_z, bands, start + REACH, start, count)
        for r in range(0, count, 2):
            one(start + r)
        return carry

    lax.fori_loop(0, (last - first) // count, chunk, 0)


def along_z(field, far_z, bands, row, i, count):
    v = field[pl.ds(row, count), :, 0:8].reshape(count * BX * 8, 128)
    far_z[pl.ds(i, count)] = band_product(v, bands).reshape(count, BX, 8, 128)


def apply(field, pot, far_z, row, pot_row, i):
    totals = [[], []]
    for begin in range(0, BX, 4):
        lines = [
            [take(field, row + r, y) for y in range(begin - REACH, begin + 4 + REACH)]
            for r in range(2)
        ]
        for yi in range(begin, begin + 4):
            e = REACH + yi - begin
            x = {0: lines[0][e], 1: lines[1][e]}
            for d in (*range(-REACH, 0), *range(2, REACH + 2)):
                x[d] = take(field, row + d, yi)
            for r in range(2):
                line = lines[r]
                total = pot[pot_row + r, yi] * line[e] + far_z[i + r, yi]
                for j in range(1, REACH + 1):
                    near = (x[r + j] + x[r - j]) + (line[e + j] + line[e - j])
                    total = total + coupling[j] * near
                totals[r].append(total)
    return totals


def put_pots(pot, mine, sources, row, skip):
    odd = iota((8, 128), 0) % 2 == 1
    for z in range(len(skip)):
        for k in range(2):
            for source, parity in zip(sources, (mine, 1 - mine)):
                at = row + z * BX + 2 * k + parity
                for yi in range(BX):
                    tile = diagonal + source[2 * z + k, yi] * (1.0 / half_width)
                    if skip[z] != 0:
                        pot[at, yi] = jnp.where(odd, pltpu.roll(tile, 1, 0), tile)
                    if skip[z] != 1:
                        pot[at + 4, yi] = jnp.where(odd, tile, pltpu.roll(tile, 7, 0))


def steps(field0, field1, field2, pot, far_z):
    def first(i):
        for r, ts in enumerate(apply(field0, pot, far_z, i + REACH, i, i)):
            put(field1, i + r, ts)

    def second(i):
        for r, ts in enumerate(apply(field1, pot, far_z, i + REACH, i + REACH, i)):
            before = i + r + FLAT
            put(field2, i + r, [t + t - take(field0, before, yi) for yi, t in enumerate(ts)])

    return first, second


def inner_kernel(core, got, mid_pot, far_mid, field0, field1, field2, pot, far_z):
    bands = band_parts()
    for z in range(4):
        def fill(xi, carry, z=z):
            put(field0, DEEP + z * BX + xi, [gather(got, z, xi, yi) for yi in range(BX)])
            return carry

        lax.fori_loop(0, BX, fill, 0)
    put_pots(pot, core[0], (mid_pot, far_mid), FLAT, (None,) * 4)
    first, second = steps(field0, field1, field2, pot, far_z)
    sweep(field0, far_z, bands, *IN1, IN1[1] - IN1[0], first)
    sweep(field1, far_z, bands, *IN2, IN2[1] - IN2[0], second)


def outer_kernel(
    core, low, high, low_pot, high_pot, far_low, far_high, _0, _1, _2, _3,
    out, field0, field1, field2, pot, far_z,
):
    bands = band_parts()

    def edge(i, carry):
        put(field0, i, [low[i, yi] for yi in range(BX)])
        put(field0, DEEP + SLAB + i, [high[i, yi] for yi in range(BX)])
        return carry

    lax.fori_loop(0, DEEP, edge, 0)
    mine = core[0]
    put_pots(pot, mine, (low_pot, far_low), FLAT - 2 * BX, (0, None))
    put_pots(pot, mine, (high_pot, far_high), FLAT + SLAB, (None, 1))
    first, second = steps(field0, field1, field2, pot, far_z)

    def third(i):
        for r, ts in enumerate(apply(field2, pot, far_z, i + REACH, i + FLAT, i)):
            for yi, t in enumerate(ts):
                start = ((i // BX) * 4 * PAIR * BX + i % BX + r) * BX + yi
                out[pl.ds(start, 8, stride=BX * BX), :] = (
                    t + t - take(field1, i + r + FLAT, yi)
                )

    ends1, ends2 = SLAB + 2 * FLAT, SLAB + FLAT
    sweep(field0, far_z, bands, 0, IN1[0], IN1[0], first)
    sweep(field0, far_z, bands, IN1[1], ends1, ends1 - IN1[1], first)
    sweep(field1, far_z, bands, 0, IN2[0], IN2[0], second)
    sweep(field1, far_z, bands, IN2[1], ends2, ends2 - IN2[1], second)
    sweep(field2, far_z, bands, 0, SLAB, SLAB // 2, third)


def iota(shape, dim):
    return lax.broadcasted_iota(jnp.int32, shape, dim)


def spread(orbital_count):
    shape = (orbital_count * BX, orbital_count)
    return (iota(shape, 0) // BX == iota(shape, 1)).astype(jnp.float32)


def same_y(orbital_count):
    shape = (orbital_count * BX, orbital_count * BX)
    return iota(shape, 0) % BX == iota(shape, 1) % BX


def dot(a, b, dims=((1,), (0,))):
    return lax.dot_general(
        a, b, (dims, ((), ())), precision=highest, preferred_element_type=jnp.float32
    )


def pair_of_rows(y, x):
    rows = y.shape[0] * BX
    return jnp.concatenate([y[:, x].reshape(rows, 128), y[:, x + 1].reshape(rows, 128)], axis=1)


def gram_kernel(scale, y, out):
    n = y.shape[0]
    total = None
    for x in range(0, BX, 2):
        block = pair_of_rows(y, x)
        part = dot(block, block, ((1,), (1,)))
        total = part if total is None else total + part
    total = jnp.where(same_y(n), total, 0.0) * scale
    ones = spread(n)
    gram = dot(dot(ones, total, ((0,), (0,))), ones)
    half = n // 2
    upper = iota((half, half), 0) <= iota((half, half), 1)
    kept = jnp.concatenate(
        [jnp.where(upper, gram[:half, :half], gram[half:, half:]), gram[:half, half:]], axis=1
    )
    unit = iota((half, half), 0) == iota((half, half), 1)
    ends = jnp.sum(jnp.where(unit, gram[half:, half:], 0.0), axis=0, keepdims=True)
    ends = jnp.concatenate([ends, jnp.zeros((1, 128 - half), jnp.float32)], axis=1)
    rows = jnp.concatenate([kept[4 * k : 4 * k + 4] for k in range(4)], axis=1)
    rows = jnp.concatenate([rows, ends], axis=0)
    for d in range(out.shape[0] // 5):
        out[5 * d : 5 * d + 5] = rows


def finish_kernel(parts, y, out, factor):
    n = y.shape[0]
    half = n // 2
    rows = []
    for r in range(5):
        total = None
        for d in range(0, parts.shape[0] // 5, 8):
            tile = parts[pl.ds(5 * d + r, 8, stride=5), :]
            total = tile if total is None else total + tile
        rows.append(jnp.sum(total, axis=0, keepdims=True))
    rows = jnp.concatenate(rows, axis=0)
    kept = jnp.concatenate([rows[:4, n * k : n * k + n] for k in range(4)], axis=0)
    across = kept[:, half:]
    unit = iota((half, half), 0) == iota((half, half), 1)
    upper = iota((half, half), 0) < iota((half, half), 1)
    mixed = kept[:, :half]
    turned = mixed.T
    first = jnp.where(upper | unit, mixed, turned)
    last = jnp.where(upper, turned, mixed)
    last = jnp.where(unit, jnp.broadcast_to(rows[4:5, :half], (half, half)), last)
    gram = jnp.concatenate(
        [jnp.concatenate([first, across], axis=1), jnp.concatenate([across.T, last], axis=1)],
        axis=0,
    )
    unit = (iota((n, n), 0) == iota((n, n), 1)).astype(jnp.float32)
    left = jnp.concatenate([gram, unit, jnp.zeros((n, 128 - 2 * n), jnp.float32)], axis=1)
    row_of = iota((n, 128), 0)
    finished = []
    for k in range(0, n, STEP):
        entry = {
            (i, j): jnp.broadcast_to(left[k + i : k + i + 1, k + j : k + j + 1], (1, 128))
            for i in range(STEP)
            for j in range(i + 1)
        }
        columns = [
            jnp.broadcast_to(left[:, k + j : k + j + 1], (n, 128)) for j in range(STEP)
        ]
        lines = [left[k + j : k + j + 1] for j in range(STEP)]
        for j in range(STEP):
            inverse = lax.rsqrt(entry[j, j])
            lines[j] = lines[j] * inverse
            columns[j] = columns[j] * inverse
            for i in range(j + 1, STEP):
                entry[i, j] = entry[i, j] * inverse
            for i in range(j + 1, STEP):
                for m in range(j + 1, i + 1):
                    entry[i, m] = entry[i, m] - entry[i, j] * entry[m, j]
                lines[i] = lines[i] - entry[i, j] * lines[j]
                columns[i] = columns[i] - entry[i, j] * columns[j]
        finished += lines
        change = None
        for line, column in zip(lines, columns):
            part = column * line
            change = part if change is None else change + part
        left = jnp.where(row_of >= k + STEP, left - change, left)
    done = jnp.concatenate(finished, axis=0)
    factor[...] = jnp.where(iota((n, n), 0) <= iota((n, n), 1), done[:, :n], 0.0)
    mixer = done[:, n : 2 * n]
    ones = spread(n)
    tall = jnp.broadcast_to(mixer[:, None], (n, BX, n)).reshape(n * BX, n)
    wide_mixer = jnp.where(same_y(n), dot(tall, ones, ((1,), (1,))), 0.0)
    for x in range(0, BX, 2):
        mixed = dot(wide_mixer, pair_of_rows(y, x))
        out[:, x] = mixed[:, :128].reshape(n, BX, 128)
        out[:, x + 1] = mixed[:, 128:].reshape(n, BX, 128)


def call(kernel, out_shape, in_specs, scratch=(), limit=8, flops=0, moved=0, aliases={}):
    return pl.pallas_call(
        kernel,
        out_shape=out_shape,
        in_specs=in_specs,
        out_specs=jax.tree.map(lambda _: VMEM, out_shape),
        scratch_shapes=list(scratch),
        input_output_aliases=aliases,
        compiler_params=pltpu.CompilerParams(vmem_limit_bytes=limit << 20),
        cost_estimate=pl.CostEstimate(flops=flops, bytes_accessed=moved, transcendentals=0),
    )


def f32(*shape):
    return jax.ShapeDtypeStruct(shape, jnp.float32)


def per_device(orbitals, potential):
    n = orbitals.shape[0]
    slabs = lax.axis_size("s")
    group = lax.axis_size("z") * lax.axis_size("gy")
    core = lax.axis_index("gy") & 1
    sent = call(
        message_kernel,
        f32(group, PAIR, BLOCK, BX, 128),
        [VMEM, VMEM],
    )(orbitals.reshape(group, PAIR, BX, BX, 128), potential)
    got = lax.all_to_all(sent, ("z", "gy"), 0, 0, tiled=True)
    got = got.reshape(group * PAIR * BLOCK * BX, 128)
    up, down, up_pot, down_pot, mid_pot = call(
        pack_kernel, (f32(DEEP, 8, 8, 128),) * 2 + (f32(4, 8, 8, 128),) * 2 + (f32(8, 8, 8, 128),), [VMEM]
    )(got)
    ring = [(i, (i + 1) % slabs) for i in range(slabs)]
    back_ring = [(j, i) for i, j in ring]
    twin = [(i, i ^ 1) for i in range(lax.axis_size("gy"))]
    low_pot = lax.ppermute(up_pot, "s", ring)
    high_pot = lax.ppermute(down_pot, "s", back_ring)
    low = lax.ppermute(up, "s", ring)
    high = lax.ppermute(down, "s", back_ring)
    far_mid = lax.ppermute(mid_pot, "gy", twin)
    own = (core.reshape(1),)
    fields = tuple(f32(rows, BX, 16, 128) for rows in (SLAB + 2 * DEEP, SLAB + 2 * FLAT, SLAB + FLAT))
    fields += (f32(SLAB + 2 * FLAT, BX, 8, 128),)
    far_z = [pltpu.VMEM((SLAB + 2 * FLAT, BX, 8, 128), jnp.float32)]
    inner = call(inner_kernel, fields, [SMEM] + [VMEM] * 3, far_z, 10, flops=1 << 32)(
        *own, got, mid_pot, far_mid
    )
    low_pot, high_pot, inner = lax.optimization_barrier((low_pot, high_pot, inner))
    far_low = lax.ppermute(low_pot, "gy", twin)
    far_high = lax.ppermute(high_pot, "gy", twin)
    filtered = call(
        outer_kernel,
        (f32(group * PAIR * BX * BX, 128),) + fields,
        [SMEM] + [VMEM] * 10,
        far_z,
        10,
        aliases={7 + k: 1 + k for k in range(4)},
    )(*own, low, high, low_pot, high_pot, far_low, far_high, *inner)[0]
    filtered = filtered.reshape(group, PAIR, BX, BX, 128)
    back = lax.all_to_all(filtered, ("z", "gy"), 0, 0, tiled=True).reshape(n, BX, BX, 128)
    devices = slabs * group
    cells = float(devices * BX * BX * 128)
    parts = call(
        functools.partial(gram_kernel, 1.0 / cells), f32(devices * 5, 128), [VMEM]
    )(back)
    parts = lax.all_to_all(
        parts.reshape(devices, 1, 5 * 128), ("s", "z", "gy"), 0, 0, tiled=True
    ).reshape(devices * 5, 128)
    return call(finish_kernel, (f32(n, BX, BX, 128), f32(n, n)), [VMEM, VMEM])(parts, back)


def solution(mesh):
    shape = mesh.devices.shape
    fine = Mesh(mesh.devices.reshape(shape[0] // 4, 4, shape[1]), ("s", "z", "gy"))
    return jax.shard_map(
        per_device,
        mesh=fine,
        in_specs=(P(None, ("s", "z"), "gy", None), P(("s", "z"), "gy", None)),
        out_specs=(P(None, ("s", "z"), "gy", None), P()),
        check_vma=False,
    )
```

```python
import functools

import jax
import jax.numpy as jnp
from jax import lax
from jax.experimental import pallas as pl
from jax.experimental.pallas import tpu as pltpu
from jax.sharding import Mesh
from jax.sharding import PartitionSpec as P

stencil_weights = (
    -5369.0 / 1800.0,
    12.0 / 7.0,
    -15.0 / 56.0,
    10.0 / 189.0,
    -1.0 / 112.0,
    2.0 / 1925.0,
    -1.0 / 16632.0,
)
grid_spacing = 0.5
filter_low = 4.0
filter_high = 46.0
centre_shift = 0.5 * (filter_high + filter_low)
half_width = 0.5 * (filter_high - filter_low)
kinetic = -0.5 / grid_spacing**2
diagonal = (kinetic * 3.0 * stencil_weights[0] - centre_shift) / half_width
coupling = tuple(kinetic * w / half_width for w in stencil_weights)
highest = lax.Precision.HIGHEST

REACH = 6
DEEP = 3 * REACH
FLAT = 2 * REACH
STEP = 4
PAIR = 2
IN1 = (DEEP, DEEP + 20)
IN2 = (DEEP, DEEP + 8)
BX = 8
BLOCK = BX + 2
SLAB = 4 * BX
VMEM = pl.BlockSpec(memory_space=pltpu.VMEM)
SMEM = pl.BlockSpec(memory_space=pltpu.SMEM)


def gather(got, z, xi, yi):
    return got[pl.ds(((z * 4) * PAIR * BLOCK + xi) * BX + yi, 8, stride=BLOCK * BX), :]


def message_kernel(orbitals, potential, out, rows, arrived):
    copy = pltpu.make_async_copy(orbitals, out.at[:, :, 0:BX], arrived.at[0])
    flat = pltpu.make_async_copy(potential, rows, arrived.at[1])
    flat.start()
    copy.start()
    flat.wait()
    for d in range(out.shape[0]):
        for o in range(PAIR):
            for k in range(2):
                out[d, o, BX + k] = rows[4 * o + 2 * k + d % 2]
    copy.wait()


def pack_kernel(got, up, down, up_pot, down_pot, mid_pot):
    for dest, first in ((up, SLAB - DEEP), (down, 0)):
        for i in range(DEEP):
            z, xi = divmod(first + i, BX)
            for yi in range(BX):
                dest[i, yi] = gather(got, z, xi, yi)
    odd = iota((8, 128), 0) % 2 == 1
    for yi in range(BX):
        tiles = [[gather(got, z, BX + k, yi) for k in range(2)] for z in range(4)]
        for z in range(4):
            for k in range(2):
                mid_pot[2 * z + k, yi] = tiles[z][k]
        up_pot[0, yi] = jnp.where(odd, tiles[2][1], pltpu.roll(tiles[2][0], 7, 0))
        down_pot[2, yi] = jnp.where(odd, pltpu.roll(tiles[1][1], 1, 0), tiles[1][0])
        for k in range(2):
            up_pot[1 + k, yi] = tiles[3][k]
            down_pot[k, yi] = tiles[0][k]


def put(field, row, tiles):
    for yi in range(BX):
        field[row, yi, 0:8] = tiles[yi]
        field[row, yi, 8:16] = tiles[yi]


def take(field, row, yi):
    first = 8 - PAIR if yi < 0 else PAIR if yi >= BX else 0
    return field[row, yi % BX, first : first + 8]


def parts_of(v):
    high = v.astype(jnp.bfloat16)
    rest = v - high.astype(jnp.float32)
    middle = rest.astype(jnp.bfloat16)
    return high, middle, (rest - middle.astype(jnp.float32)).astype(jnp.bfloat16)


def band_parts():
    apart = (iota((128, 128), 0) - iota((128, 128), 1)) % 128
    band = jnp.zeros((128, 128), jnp.float32)
    for j in range(1, REACH + 1):
        band = jnp.where((apart == j) | (apart == 128 - j), coupling[j], band)
    high, middle, low = parts_of(band)
    top = jnp.concatenate([high, middle], axis=1)
    return jnp.concatenate([top, top], axis=0)


def band_product(v, bands):
    high, middle, _ = parts_of(v)
    both = jnp.dot(
        jnp.concatenate([high, middle], axis=1), bands, preferred_element_type=jnp.float32
    )
    return both[:, :128] + both[:, 128:]


def sweep(field, far_z, bands, first, last, count, one):
    def chunk(c, carry):
        start = first + c * count
        along_z(field, far_z, bands, start + REACH, start, count)
        for r in range(0, count, 2):
            one(start + r)
        return carry

    lax.fori_loop(0, (last - first) // count, chunk, 0)


def along_z(field, far_z, bands, row, i, count):
    v = field[pl.ds(row, count), :, 0:8].reshape(count * BX * 8, 128)
    far_z[pl.ds(i, count)] = band_product(v, bands).reshape(count, BX, 8, 128)


def apply(field, pot, far_z, row, pot_row, i):
    totals = [[], []]
    for begin in range(0, BX, 4):
        lines = [
            [take(field, row + r, y) for y in range(begin - REACH, begin + 4 + REACH)]
            for r in range(2)
        ]
        for yi in range(begin, begin + 4):
            e = REACH + yi - begin
            x = {0: lines[0][e], 1: lines[1][e]}
            for d in (*range(-REACH, 0), *range(2, REACH + 2)):
                x[d] = take(field, row + d, yi)
            for r in range(2):
                line = lines[r]
                total = pot[pot_row + r, yi] * line[e] + far_z[i + r, yi]
                for j in range(1, REACH + 1):
                    near = (x[r + j] + x[r - j]) + (line[e + j] + line[e - j])
                    total = total + coupling[j] * near
                totals[r].append(total)
    return totals


WHOLE = tuple((8 * z + 2 * k, 8 * z + 2 * k + 4) for z in range(4) for k in range(2))


def put_pots(pot, mine, sources, slots, row):
    odd = iota((8, 128), 0) % 2 == 1
    for slot, (even_row, odd_row) in enumerate(slots):
        for source, parity in zip(sources, (mine, 1 - mine)):
            for yi in range(BX):
                tile = diagonal + source[slot, yi] * (1.0 / half_width)
                pot[row + even_row + parity, yi] = jnp.where(odd, pltpu.roll(tile, 1, 0), tile)
                pot[row + odd_row + parity, yi] = jnp.where(odd, tile, pltpu.roll(tile, 7, 0))


def steps(field0, field1, field2, pot, far_z):
    def first(i):
        for r, ts in enumerate(apply(field0, pot, far_z, i + REACH, i, i)):
            put(field1, i + r, ts)

    def second(i):
        for r, ts in enumerate(apply(field1, pot, far_z, i + REACH, i + REACH, i)):
            before = i + r + FLAT
            put(field2, i + r, [t + t - take(field0, before, yi) for yi, t in enumerate(ts)])

    return first, second


def inner_kernel(core, got, mid_pot, far_mid, field0, field1, field2, pot, far_z):
    bands = band_parts()
    for z in range(4):
        def fill(xi, carry, z=z):
            put(field0, DEEP + z * BX + xi, [gather(got, z, xi, yi) for yi in range(BX)])
            return carry

        lax.fori_loop(0, BX, fill, 0)
    put_pots(pot, core[0], (mid_pot, far_mid), WHOLE, FLAT)
    first, second = steps(field0, field1, field2, pot, far_z)
    sweep(field0, far_z, bands, *IN1, IN1[1] - IN1[0], first)
    sweep(field1, far_z, bands, *IN2, IN2[1] - IN2[0], second)


def edge_kernel(low, high, _, field0, far_z):
    bands = band_parts()

    def edge(i, carry):
        put(field0, i, [low[i, yi] for yi in range(BX)])
        put(field0, DEEP + SLAB + i, [high[i, yi] for yi in range(BX)])
        return carry

    lax.fori_loop(0, DEEP, edge, 0)
    along_z(field0, far_z, bands, REACH, 0, IN1[0])
    along_z(field0, far_z, bands, REACH + IN1[1], IN1[1], SLAB + 2 * FLAT - IN1[1])


def outer_kernel(
    core, low_pot, high_pot, far_low, far_high, field0, _1, _2, _3, _4,
    out, field1, field2, pot, far_z,
):
    bands = band_parts()
    mine = core[0]
    put_pots(pot, mine, (low_pot, far_low), ((0, 2), (4, 8), (6, 10)), 0)
    put_pots(pot, mine, (high_pot, far_high), ((0, 4), (2, 6), (8, 10)), FLAT + SLAB)
    first, second = steps(field0, field1, field2, pot, far_z)

    def third(i):
        for r, ts in enumerate(apply(field2, pot, far_z, i + REACH, i + FLAT, i)):
            for yi, t in enumerate(ts):
                start = ((i // BX) * 4 * PAIR * BX + i % BX + r) * BX + yi
                out[pl.ds(start, 8, stride=BX * BX), :] = (
                    t + t - take(field1, i + r + FLAT, yi)
                )

    ends1, ends2 = SLAB + 2 * FLAT, SLAB + FLAT
    for begin, end in ((0, IN1[0]), (IN1[1], ends1)):
        for r in range(begin, end, 2):
            first(r)
    sweep(field1, far_z, bands, 0, IN2[0], IN2[0], second)
    sweep(field1, far_z, bands, IN2[1], ends2, ends2 - IN2[1], second)
    sweep(field2, far_z, bands, 0, SLAB, SLAB // 2, third)


def iota(shape, dim):
    return lax.broadcasted_iota(jnp.int32, shape, dim)


def spread(orbital_count):
    shape = (orbital_count * BX, orbital_count)
    return (iota(shape, 0) // BX == iota(shape, 1)).astype(jnp.float32)


def same_y(orbital_count):
    shape = (orbital_count * BX, orbital_count * BX)
    return iota(shape, 0) % BX == iota(shape, 1) % BX


def dot(a, b, dims=((1,), (0,))):
    return lax.dot_general(
        a, b, (dims, ((), ())), precision=highest, preferred_element_type=jnp.float32
    )


def pair_of_rows(y, x):
    rows = y.shape[0] * BX
    return jnp.concatenate([y[:, x].reshape(rows, 128), y[:, x + 1].reshape(rows, 128)], axis=1)


def gram_kernel(scale, y, out):
    n = y.shape[0]
    total = None
    for x in range(0, BX, 2):
        block = pair_of_rows(y, x)
        part = dot(block, block, ((1,), (1,)))
        total = part if total is None else total + part
    total = jnp.where(same_y(n), total, 0.0) * scale
    ones = spread(n)
    gram = dot(dot(ones, total, ((0,), (0,))), ones)
    half = n // 2
    upper = iota((half, half), 0) <= iota((half, half), 1)
    kept = jnp.concatenate(
        [jnp.where(upper, gram[:half, :half], gram[half:, half:]), gram[:half, half:]], axis=1
    )
    unit = iota((half, half), 0) == iota((half, half), 1)
    ends = jnp.sum(jnp.where(unit, gram[half:, half:], 0.0), axis=0, keepdims=True)
    ends = jnp.concatenate([ends, jnp.zeros((1, 128 - half), jnp.float32)], axis=1)
    rows = jnp.concatenate([kept[4 * k : 4 * k + 4] for k in range(4)], axis=1)
    rows = jnp.concatenate([rows, ends], axis=0)
    for d in range(out.shape[0] // 5):
        out[5 * d : 5 * d + 5] = rows


def finish_kernel(parts, y, out, factor):
    n = y.shape[0]
    half = n // 2
    rows = []
    for r in range(5):
        total = None
        for d in range(0, parts.shape[0] // 5, 8):
            tile = parts[pl.ds(5 * d + r, 8, stride=5), :]
            total = tile if total is None else total + tile
        rows.append(jnp.sum(total, axis=0, keepdims=True))
    rows = jnp.concatenate(rows, axis=0)
    kept = jnp.concatenate([rows[:4, n * k : n * k + n] for k in range(4)], axis=0)
    across = kept[:, half:]
    unit = iota((half, half), 0) == iota((half, half), 1)
    upper = iota((half, half), 0) < iota((half, half), 1)
    mixed = kept[:, :half]
    turned = mixed.T
    first = jnp.where(upper | unit, mixed, turned)
    last = jnp.where(upper, turned, mixed)
    last = jnp.where(unit, jnp.broadcast_to(rows[4:5, :half], (half, half)), last)
    gram = jnp.concatenate(
        [jnp.concatenate([first, across], axis=1), jnp.concatenate([across.T, last], axis=1)],
        axis=0,
    )
    unit = (iota((n, n), 0) == iota((n, n), 1)).astype(jnp.float32)
    left = jnp.concatenate([gram, unit, jnp.zeros((n, 128 - 2 * n), jnp.float32)], axis=1)
    row_of = iota((n, 128), 0)
    finished = []
    for k in range(0, n, STEP):
        entry = {
            (i, j): jnp.broadcast_to(left[k + i : k + i + 1, k + j : k + j + 1], (1, 128))
            for i in range(STEP)
            for j in range(i + 1)
        }
        columns = [
            jnp.broadcast_to(left[:, k + j : k + j + 1], (n, 128)) for j in range(STEP)
        ]
        lines = [left[k + j : k + j + 1] for j in range(STEP)]
        for j in range(STEP):
            inverse = lax.rsqrt(entry[j, j])
            lines[j] = lines[j] * inverse
            columns[j] = columns[j] * inverse
            for i in range(j + 1, STEP):
                entry[i, j] = entry[i, j] * inverse
            for i in range(j + 1, STEP):
                for m in range(j + 1, i + 1):
                    entry[i, m] = entry[i, m] - entry[i, j] * entry[m, j]
                lines[i] = lines[i] - entry[i, j] * lines[j]
                columns[i] = columns[i] - entry[i, j] * columns[j]
        finished += lines
        change = None
        for line, column in zip(lines, columns):
            part = column * line
            change = part if change is None else change + part
        left = jnp.where(row_of >= k + STEP, left - change, left)
    done = jnp.concatenate(finished, axis=0)
    factor[...] = jnp.where(iota((n, n), 0) <= iota((n, n), 1), done[:, :n], 0.0)
    mixer = done[:, n : 2 * n]
    ones = spread(n)
    tall = jnp.broadcast_to(mixer[:, None], (n, BX, n)).reshape(n * BX, n)
    wide_mixer = jnp.where(same_y(n), dot(tall, ones, ((1,), (1,))), 0.0)
    for x in range(0, BX, 2):
        mixed = dot(wide_mixer, pair_of_rows(y, x))
        out[:, x] = mixed[:, :128].reshape(n, BX, 128)
        out[:, x + 1] = mixed[:, 128:].reshape(n, BX, 128)


def call(kernel, out_shape, in_specs, scratch=(), limit=8, flops=0, moved=0, aliases={}):
    return pl.pallas_call(
        kernel,
        out_shape=out_shape,
        in_specs=in_specs,
        out_specs=jax.tree.map(lambda _: VMEM, out_shape),
        scratch_shapes=list(scratch),
        input_output_aliases=aliases,
        compiler_params=pltpu.CompilerParams(vmem_limit_bytes=limit << 20),
        cost_estimate=pl.CostEstimate(flops=flops, bytes_accessed=moved, transcendentals=0),
    )


def f32(*shape):
    return jax.ShapeDtypeStruct(shape, jnp.float32)


def per_device(orbitals, potential):
    n = orbitals.shape[0]
    slabs = lax.axis_size("s")
    group = lax.axis_size("z") * lax.axis_size("gy")
    core = lax.axis_index("gy") & 1
    away = pl.BlockSpec(memory_space=pltpu.HBM)
    sent = call(
        message_kernel,
        f32(group, PAIR, BLOCK, BX, 128),
        [away, away],
        [pltpu.VMEM((BX, BX, 128), jnp.float32), pltpu.SemaphoreType.DMA((2,))],
    )(
        pltpu.with_memory_space_constraint(orbitals.reshape(group, PAIR, BX, BX, 128), pltpu.HBM),
        pltpu.with_memory_space_constraint(potential, pltpu.HBM),
    )
    got = lax.all_to_all(sent, ("z", "gy"), 0, 0, tiled=True)
    got = got.reshape(group * PAIR * BLOCK * BX, 128)
    up, down, up_pot, down_pot, mid_pot = call(
        pack_kernel, (f32(DEEP, 8, 8, 128),) * 2 + (f32(3, 8, 8, 128),) * 2 + (f32(8, 8, 8, 128),), [VMEM]
    )(got)
    ring = [(i, (i + 1) % slabs) for i in range(slabs)]
    back_ring = [(j, i) for i, j in ring]
    twin = [(i, i ^ 1) for i in range(lax.axis_size("gy"))]
    low_pot = lax.ppermute(up_pot, "s", ring)
    high_pot = lax.ppermute(down_pot, "s", back_ring)
    low = lax.ppermute(up, "s", ring)
    high = lax.ppermute(down, "s", back_ring)
    far_mid = lax.ppermute(mid_pot, "gy", twin)
    own = (core.reshape(1),)
    fields = tuple(f32(rows, BX, 16, 128) for rows in (SLAB + 2 * DEEP, SLAB + 2 * FLAT, SLAB + FLAT))
    fields += (f32(SLAB + 2 * FLAT, BX, 8, 128),)
    far_z = [pltpu.VMEM((SLAB + 2 * FLAT, BX, 8, 128), jnp.float32)]
    inner = call(inner_kernel, fields, [SMEM] + [VMEM] * 3, far_z, 10, flops=1 << 32)(
        *own, got, mid_pot, far_mid
    )
    low_pot, high_pot, inner = lax.optimization_barrier((low_pot, high_pot, inner))
    far_low = lax.ppermute(low_pot, "gy", twin)
    far_high = lax.ppermute(high_pot, "gy", twin)
    field0, field1, field2, pot = inner
    field0, products = call(
        edge_kernel, (fields[0], fields[3]), [VMEM] * 3, (), 10, flops=1 << 30, aliases={2: 0}
    )(low, high, field0)
    filtered = call(
        outer_kernel,
        (f32(group * PAIR * BX * BX, 128),) + fields[1:] + (fields[3],),
        [SMEM] + [VMEM] * 9,
        (),
        10,
        aliases={6 + k: 1 + k for k in range(4)},
    )(*own, low_pot, high_pot, far_low, far_high, field0, field1, field2, pot, products)[0]
    filtered = filtered.reshape(group, PAIR, BX, BX, 128)
    back = lax.all_to_all(filtered, ("z", "gy"), 0, 0, tiled=True).reshape(n, BX, BX, 128)
    devices = slabs * group
    cells = float(devices * BX * BX * 128)
    parts = call(
        functools.partial(gram_kernel, 1.0 / cells), f32(devices * 5, 128), [VMEM]
    )(back)
    parts = lax.all_to_all(
        parts.reshape(devices, 1, 5 * 128), ("s", "z", "gy"), 0, 0, tiled=True
    ).reshape(devices * 5, 128)
    return call(finish_kernel, (f32(n, BX, BX, 128), f32(n, n)), [VMEM, VMEM])(parts, back)


def solution(mesh):
    shape = mesh.devices.shape
    fine = Mesh(mesh.devices.reshape(shape[0] // 4, 4, shape[1]), ("s", "z", "gy"))
    return jax.shard_map(
        per_device,
        mesh=fine,
        in_specs=(P(None, ("s", "z"), "gy", None), P(("s", "z"), "gy", None)),
        out_specs=(P(None, ("s", "z"), "gy", None), P()),
        check_vma=False,
    )
```

```python
import functools

import jax
import jax.numpy as jnp
from jax import lax
from jax.experimental import pallas as pl
from jax.experimental.pallas import tpu as pltpu
from jax.sharding import Mesh
from jax.sharding import PartitionSpec as P

stencil_weights = (
    -5369.0 / 1800.0,
    12.0 / 7.0,
    -15.0 / 56.0,
    10.0 / 189.0,
    -1.0 / 112.0,
    2.0 / 1925.0,
    -1.0 / 16632.0,
)
grid_spacing = 0.5
filter_low = 4.0
filter_high = 46.0
centre_shift = 0.5 * (filter_high + filter_low)
half_width = 0.5 * (filter_high - filter_low)
kinetic = -0.5 / grid_spacing**2
diagonal = (kinetic * 3.0 * stencil_weights[0] - centre_shift) / half_width
coupling = tuple(kinetic * w / half_width for w in stencil_weights)
highest = lax.Precision.HIGHEST

REACH = 6
DEEP = 3 * REACH
FLAT = 2 * REACH
FLOWS = 4
STEP = 4
PAIR = 2
IN1 = (DEEP, DEEP + 20)
IN2 = (DEEP, DEEP + 8)
BX = 8
BLOCK = BX + 2
SLAB = 4 * BX
VMEM = pl.BlockSpec(memory_space=pltpu.VMEM)
SMEM = pl.BlockSpec(memory_space=pltpu.SMEM)


def gather(got, z, xi, yi):
    return got[pl.ds(((z * 4) * PAIR * BLOCK + xi) * BX + yi, 8, stride=BLOCK * BX), :]


def message_kernel(orbitals, potential, out, rows, arrived):
    flat = pltpu.make_async_copy(potential, rows, arrived.at[FLOWS])
    flat.start()
    part = out.shape[0] // FLOWS
    copies = []
    for f in range(FLOWS):
        some = pl.ds(f * part, part)
        copies.append(
            pltpu.make_async_copy(orbitals.at[some], out.at[some, :, 0:BX], arrived.at[f])
        )
        copies[-1].start()
    flat.wait()
    for d in range(out.shape[0]):
        for o in range(PAIR):
            for k in range(2):
                out[d, o, BX + k] = rows[4 * o + 2 * k + d % 2]
    for copy in copies:
        copy.wait()


def pack_kernel(got, up, down, mid_pot):
    for dest, first in ((up, SLAB - DEEP), (down, 0)):
        for i in range(DEEP):
            z, xi = divmod(first + i, BX)
            for yi in range(BX):
                dest[i, yi] = gather(got, z, xi, yi)
    odd = iota((8, 128), 0) % 2 == 1
    for yi in range(BX):
        tiles = [[gather(got, z, BX + k, yi) for k in range(2)] for z in range(4)]
        for z in range(4):
            for k in range(2):
                mid_pot[2 * z + k, yi] = tiles[z][k]
        up[DEEP, yi] = jnp.where(odd, tiles[2][1], pltpu.roll(tiles[2][0], 7, 0))
        down[DEEP + 2, yi] = jnp.where(odd, pltpu.roll(tiles[1][1], 1, 0), tiles[1][0])
        for k in range(2):
            up[DEEP + 1 + k, yi] = tiles[3][k]
            down[DEEP + k, yi] = tiles[0][k]


def put(field, row, tiles):
    for yi in range(BX):
        field[row, yi, 0:8] = tiles[yi]
        field[row, yi, 8:16] = tiles[yi]


def take(field, row, yi):
    first = 8 - PAIR if yi < 0 else PAIR if yi >= BX else 0
    return field[row, yi % BX, first : first + 8]


def parts_of(v):
    high = v.astype(jnp.bfloat16)
    rest = v - high.astype(jnp.float32)
    middle = rest.astype(jnp.bfloat16)
    return high, middle, (rest - middle.astype(jnp.float32)).astype(jnp.bfloat16)


def band_parts():
    apart = (iota((128, 128), 0) - iota((128, 128), 1)) % 128
    band = jnp.zeros((128, 128), jnp.float32)
    for j in range(1, REACH + 1):
        band = jnp.where((apart == j) | (apart == 128 - j), coupling[j], band)
    high, middle, low = parts_of(band)
    top = jnp.concatenate([high, middle], axis=1)
    return jnp.concatenate([top, top], axis=0)


def band_product(v, bands):
    high, middle, _ = parts_of(v)
    both = jnp.dot(
        jnp.concatenate([high, middle], axis=1), bands, preferred_element_type=jnp.float32
    )
    return both[:, :128] + both[:, 128:]


def sweep(field, far_z, bands, first, last, count, one):
    def chunk(c, carry):
        start = first + c * count
        along_z(field, far_z, bands, start + REACH, start, count)
        for r in range(0, count, 2):
            one(start + r)
        return carry

    lax.fori_loop(0, (last - first) // count, chunk, 0)


def along_z(field, far_z, bands, row, i, count):
    v = field[pl.ds(row, count), :, 0:8].reshape(count * BX * 8, 128)
    far_z[pl.ds(i, count)] = band_product(v, bands).reshape(count, BX, 8, 128)


def apply(field, pot, far_z, row, pot_row, i):
    totals = [[], []]
    for begin in range(0, BX, 4):
        lines = [
            [take(field, row + r, y) for y in range(begin - REACH, begin + 4 + REACH)]
            for r in range(2)
        ]
        for yi in range(begin, begin + 4):
            e = REACH + yi - begin
            x = {0: lines[0][e], 1: lines[1][e]}
            for d in (*range(-REACH, 0), *range(2, REACH + 2)):
                x[d] = take(field, row + d, yi)
            for r in range(2):
                line = lines[r]
                total = pot[pot_row + r, yi] * line[e] + far_z[i + r, yi]
                for j in range(1, REACH + 1):
                    near = (x[r + j] + x[r - j]) + (line[e + j] + line[e - j])
                    total = total + coupling[j] * near
                totals[r].append(total)
    return totals


WHOLE = tuple((8 * z + 2 * k, 8 * z + 2 * k + 4) for z in range(4) for k in range(2))


def put_pots(pot, mine, sources, slots, row):
    odd = iota((8, 128), 0) % 2 == 1
    for slot, (even_row, odd_row) in enumerate(slots):
        for source, parity in zip(sources, (mine, 1 - mine)):
            for yi in range(BX):
                tile = diagonal + source[slot, yi] * (1.0 / half_width)
                pot[row + even_row + parity, yi] = jnp.where(odd, pltpu.roll(tile, 1, 0), tile)
                pot[row + odd_row + parity, yi] = jnp.where(odd, tile, pltpu.roll(tile, 7, 0))


def steps(field0, field1, field2, pot, far_z):
    def first(i):
        for r, ts in enumerate(apply(field0, pot, far_z, i + REACH, i, i)):
            put(field1, i + r, ts)

    def second(i):
        for r, ts in enumerate(apply(field1, pot, far_z, i + REACH, i + REACH, i)):
            before = i + r + FLAT
            put(field2, i + r, [t + t - take(field0, before, yi) for yi, t in enumerate(ts)])

    return first, second


def inner_kernel(core, got, mid_pot, far_mid, field0, field1, field2, pot, far_z):
    bands = band_parts()
    for z in range(4):
        def fill(xi, carry, z=z):
            put(field0, DEEP + z * BX + xi, [gather(got, z, xi, yi) for yi in range(BX)])
            return carry

        lax.fori_loop(0, BX, fill, 0)
    put_pots(pot, core[0], (mid_pot, far_mid), WHOLE, FLAT)
    first, second = steps(field0, field1, field2, pot, far_z)
    sweep(field0, far_z, bands, *IN1, IN1[1] - IN1[0], first)
    sweep(field1, far_z, bands, *IN2, IN2[1] - IN2[0], second)


def pots_kernel(low, high, low_pot, high_pot):
    low_pot[...] = low[DEEP:]
    high_pot[...] = high[DEEP:]


def edge_kernel(low, high, _, field0, far_z):
    bands = band_parts()

    def edge(i, carry):
        put(field0, i, [low[i, yi] for yi in range(BX)])
        put(field0, DEEP + SLAB + i, [high[i, yi] for yi in range(BX)])
        return carry

    lax.fori_loop(0, DEEP, edge, 0)
    along_z(field0, far_z, bands, REACH, 0, IN1[0])
    along_z(field0, far_z, bands, REACH + IN1[1], IN1[1], SLAB + 2 * FLAT - IN1[1])


def outer_kernel(
    core, low_pot, high_pot, far_low, far_high, field0, _1, _2, _3, _4,
    out, field1, field2, pot, far_z,
):
    bands = band_parts()
    mine = core[0]
    put_pots(pot, mine, (low_pot, far_low), ((0, 2), (4, 8), (6, 10)), 0)
    put_pots(pot, mine, (high_pot, far_high), ((0, 4), (2, 6), (8, 10)), FLAT + SLAB)
    first, second = steps(field0, field1, field2, pot, far_z)

    def third(i):
        for r, ts in enumerate(apply(field2, pot, far_z, i + REACH, i + FLAT, i)):
            for yi, t in enumerate(ts):
                start = ((i // BX) * 4 * PAIR * BX + i % BX + r) * BX + yi
                out[pl.ds(start, 8, stride=BX * BX), :] = (
                    t + t - take(field1, i + r + FLAT, yi)
                )

    ends1, ends2 = SLAB + 2 * FLAT, SLAB + FLAT
    for begin, end in ((0, IN1[0]), (IN1[1], ends1)):
        for r in range(begin, end, 2):
            first(r)
    sweep(field1, far_z, bands, 0, IN2[0], IN2[0], second)
    sweep(field1, far_z, bands, IN2[1], ends2, ends2 - IN2[1], second)
    sweep(field2, far_z, bands, 0, SLAB, SLAB // 2, third)


def iota(shape, dim):
    return lax.broadcasted_iota(jnp.int32, shape, dim)


def spread(orbital_count):
    shape = (orbital_count * BX, orbital_count)
    return (iota(shape, 0) // BX == iota(shape, 1)).astype(jnp.float32)


def same_y(orbital_count):
    shape = (orbital_count * BX, orbital_count * BX)
    return iota(shape, 0) % BX == iota(shape, 1) % BX


def dot(a, b, dims=((1,), (0,))):
    return lax.dot_general(
        a, b, (dims, ((), ())), precision=highest, preferred_element_type=jnp.float32
    )


def pair_of_rows(y, x):
    rows = y.shape[0] * BX
    return jnp.concatenate([y[:, x].reshape(rows, 128), y[:, x + 1].reshape(rows, 128)], axis=1)


def across(a, b):
    return lax.dot_general(a, b, (((1,), (1,)), ((), ())), preferred_element_type=jnp.float32)


def gram_kernel(scale, y, out):
    n = y.shape[0]
    total = None
    for x in range(0, BX, 2):
        high, middle, low = parts_of(pair_of_rows(y, x))
        part = 0.5 * (across(high, high) + across(middle, middle))
        part = part + (across(high, middle) + across(high, low))
        total = part if total is None else total + part
    total = jnp.where(same_y(n), total, 0.0) * scale
    ones = spread(n)
    gram = dot(dot(ones, total, ((0,), (0,))), ones)
    gram = gram + gram.T
    half = n // 2
    upper = iota((half, half), 0) <= iota((half, half), 1)
    kept = jnp.concatenate(
        [jnp.where(upper, gram[:half, :half], gram[half:, half:]), gram[:half, half:]], axis=1
    )
    unit = iota((half, half), 0) == iota((half, half), 1)
    ends = jnp.sum(jnp.where(unit, gram[half:, half:], 0.0), axis=0, keepdims=True)
    ends = jnp.concatenate([ends, jnp.zeros((1, 128 - half), jnp.float32)], axis=1)
    rows = jnp.concatenate([kept[4 * k : 4 * k + 4] for k in range(4)], axis=1)
    rows = jnp.concatenate([rows, ends], axis=0)
    for d in range(out.shape[0] // 5):
        out[5 * d : 5 * d + 5] = rows


def finish_kernel(parts, y, out, factor):
    n = y.shape[0]
    half = n // 2
    rows = []
    for r in range(5):
        total = None
        for d in range(0, parts.shape[0] // 5, 8):
            tile = parts[pl.ds(5 * d + r, 8, stride=5), :]
            total = tile if total is None else total + tile
        rows.append(jnp.sum(total, axis=0, keepdims=True))
    rows = jnp.concatenate(rows, axis=0)
    kept = jnp.concatenate([rows[:4, n * k : n * k + n] for k in range(4)], axis=0)
    across = kept[:, half:]
    unit = iota((half, half), 0) == iota((half, half), 1)
    upper = iota((half, half), 0) < iota((half, half), 1)
    mixed = kept[:, :half]
    turned = mixed.T
    first = jnp.where(upper | unit, mixed, turned)
    last = jnp.where(upper, turned, mixed)
    last = jnp.where(unit, jnp.broadcast_to(rows[4:5, :half], (half, half)), last)
    gram = jnp.concatenate(
        [jnp.concatenate([first, across], axis=1), jnp.concatenate([across.T, last], axis=1)],
        axis=0,
    )
    unit = (iota((n, n), 0) == iota((n, n), 1)).astype(jnp.float32)
    left = jnp.concatenate([gram, unit, jnp.zeros((n, 128 - 2 * n), jnp.float32)], axis=1)
    row_of = iota((n, 128), 0)
    finished = []
    for k in range(0, n, STEP):
        entry = {
            (i, j): jnp.broadcast_to(left[k + i : k + i + 1, k + j : k + j + 1], (1, 128))
            for i in range(STEP)
            for j in range(i + 1)
        }
        columns = [
            jnp.broadcast_to(left[:, k + j : k + j + 1], (n, 128)) for j in range(STEP)
        ]
        lines = [left[k + j : k + j + 1] for j in range(STEP)]
        for j in range(STEP):
            inverse = lax.rsqrt(entry[j, j])
            lines[j] = lines[j] * inverse
            columns[j] = columns[j] * inverse
            for i in range(j + 1, STEP):
                entry[i, j] = entry[i, j] * inverse
            for i in range(j + 1, STEP):
                for m in range(j + 1, i + 1):
                    entry[i, m] = entry[i, m] - entry[i, j] * entry[m, j]
                lines[i] = lines[i] - entry[i, j] * lines[j]
                columns[i] = columns[i] - entry[i, j] * columns[j]
        finished += lines
        change = None
        for line, column in zip(lines, columns):
            part = column * line
            change = part if change is None else change + part
        left = jnp.where(row_of >= k + STEP, left - change, left)
    done = jnp.concatenate(finished, axis=0)
    factor[...] = jnp.where(iota((n, n), 0) <= iota((n, n), 1), done[:, :n], 0.0)
    mixer = done[:, n : 2 * n]
    ones = spread(n)
    tall = jnp.broadcast_to(mixer[:, None], (n, BX, n)).reshape(n * BX, n)
    wide_mixer = jnp.where(same_y(n), dot(tall, ones, ((1,), (1,))), 0.0)
    for x in range(0, BX, 2):
        mixed = dot(wide_mixer, pair_of_rows(y, x))
        out[:, x] = mixed[:, :128].reshape(n, BX, 128)
        out[:, x + 1] = mixed[:, 128:].reshape(n, BX, 128)


def call(kernel, out_shape, in_specs, scratch=(), limit=8, flops=0, moved=0, aliases={}):
    return pl.pallas_call(
        kernel,
        out_shape=out_shape,
        in_specs=in_specs,
        out_specs=jax.tree.map(lambda _: VMEM, out_shape),
        scratch_shapes=list(scratch),
        input_output_aliases=aliases,
        compiler_params=pltpu.CompilerParams(vmem_limit_bytes=limit << 20),
        cost_estimate=pl.CostEstimate(flops=flops, bytes_accessed=moved, transcendentals=0),
    )


def f32(*shape):
    return jax.ShapeDtypeStruct(shape, jnp.float32)


def per_device(orbitals, potential):
    n = orbitals.shape[0]
    slabs = lax.axis_size("s")
    group = lax.axis_size("z") * lax.axis_size("gy")
    core = lax.axis_index("gy") & 1
    away = pl.BlockSpec(memory_space=pltpu.HBM)
    sent = call(
        message_kernel,
        f32(group, PAIR, BLOCK, BX, 128),
        [away, away],
        [pltpu.VMEM((BX, BX, 128), jnp.float32), pltpu.SemaphoreType.DMA((FLOWS + 1,))],
    )(
        pltpu.with_memory_space_constraint(orbitals.reshape(group, PAIR, BX, BX, 128), pltpu.HBM),
        pltpu.with_memory_space_constraint(potential, pltpu.HBM),
    )
    got = lax.all_to_all(sent, ("z", "gy"), 0, 0, tiled=True)
    got = got.reshape(group * PAIR * BLOCK * BX, 128)
    up, down, mid_pot = call(
        pack_kernel, (f32(DEEP + 3, 8, 8, 128),) * 2 + (f32(8, 8, 8, 128),), [VMEM]
    )(got)
    ring = [(i, (i + 1) % slabs) for i in range(slabs)]
    back_ring = [(j, i) for i, j in ring]
    twin = [(i, i ^ 1) for i in range(lax.axis_size("gy"))]
    low = lax.ppermute(up, "s", ring)
    high = lax.ppermute(down, "s", back_ring)
    far_mid = lax.ppermute(mid_pot, "gy", twin)
    own = (core.reshape(1),)
    fields = tuple(f32(rows, BX, 16, 128) for rows in (SLAB + 2 * DEEP, SLAB + 2 * FLAT, SLAB + FLAT))
    fields += (f32(SLAB + 2 * FLAT, BX, 8, 128),)
    far_z = [pltpu.VMEM((SLAB + 2 * FLAT, BX, 8, 128), jnp.float32)]
    inner = call(inner_kernel, fields, [SMEM] + [VMEM] * 3, far_z, 10, flops=1 << 32)(
        *own, got, mid_pot, far_mid
    )
    low, high, inner = lax.optimization_barrier((low, high, inner))
    low_pot, high_pot = call(pots_kernel, (f32(3, 8, 8, 128),) * 2, [VMEM] * 2)(low, high)
    far_low = lax.ppermute(low_pot, "gy", twin)
    far_high = lax.ppermute(high_pot, "gy", twin)
    field0, field1, field2, pot = inner
    field0, products = call(
        edge_kernel, (fields[0], fields[3]), [VMEM] * 3, (), 10, flops=1 << 30, aliases={2: 0}
    )(low, high, field0)
    filtered = call(
        outer_kernel,
        (f32(group * PAIR * BX * BX, 128),) + fields[1:] + (fields[3],),
        [SMEM] + [VMEM] * 9,
        (),
        10,
        aliases={6 + k: 1 + k for k in range(4)},
    )(*own, low_pot, high_pot, far_low, far_high, field0, field1, field2, pot, products)[0]
    filtered = filtered.reshape(group, PAIR, BX, BX, 128)
    back = lax.all_to_all(filtered, ("z", "gy"), 0, 0, tiled=True).reshape(n, BX, BX, 128)
    devices = slabs * group
    cells = float(devices * BX * BX * 128)
    parts = call(
        functools.partial(gram_kernel, 1.0 / cells), f32(devices * 5, 128), [VMEM]
    )(back)
    parts = lax.all_to_all(
        parts.reshape(devices, 1, 5 * 128), ("gy", "z", "s"), 0, 0, tiled=True
    ).reshape(devices * 5, 128)
    return call(finish_kernel, (f32(n, BX, BX, 128), f32(n, n)), [VMEM, VMEM])(parts, back)


def solution(mesh):
    shape = mesh.devices.shape
    fine = Mesh(mesh.devices.reshape(shape[0] // 4, 4, shape[1]), ("s", "z", "gy"))
    return jax.shard_map(
        per_device,
        mesh=fine,
        in_specs=(P(None, ("s", "z"), "gy", None), P(("s", "z"), "gy", None)),
        out_specs=(P(None, ("s", "z"), "gy", None), P()),
        check_vma=False,
    )
```

```python
import functools

import jax
import jax.numpy as jnp
from jax import lax
from jax.experimental import pallas as pl
from jax.experimental.pallas import tpu as pltpu
from jax.sharding import Mesh
from jax.sharding import PartitionSpec as P

stencil_weights = (
    -5369.0 / 1800.0,
    12.0 / 7.0,
    -15.0 / 56.0,
    10.0 / 189.0,
    -1.0 / 112.0,
    2.0 / 1925.0,
    -1.0 / 16632.0,
)
grid_spacing = 0.5
filter_low = 4.0
filter_high = 46.0
centre_shift = 0.5 * (filter_high + filter_low)
half_width = 0.5 * (filter_high - filter_low)
kinetic = -0.5 / grid_spacing**2
diagonal = (kinetic * 3.0 * stencil_weights[0] - centre_shift) / half_width
coupling = tuple(kinetic * w / half_width for w in stencil_weights)
highest = lax.Precision.HIGHEST

REACH = 6
DEEP = 3 * REACH
FLAT = 2 * REACH
FLOWS = 4
STEP = 8
PAIR = 2
IN1 = (DEEP, DEEP + 20)
IN2 = (DEEP, DEEP + 8)
BX = 8
BLOCK = BX + 2
SLAB = 4 * BX
VMEM = pl.BlockSpec(memory_space=pltpu.VMEM)
SMEM = pl.BlockSpec(memory_space=pltpu.SMEM)


def gather(got, z, xi, yi):
    return got[pl.ds(((z * 4) * PAIR * BLOCK + xi) * BX + yi, 8, stride=BLOCK * BX), :]


def message_kernel(orbitals, potential, out, rows, arrived):
    flat = pltpu.make_async_copy(potential, rows, arrived.at[FLOWS])
    flat.start()
    part = out.shape[0] // FLOWS
    copies = []
    for f in range(FLOWS):
        some = pl.ds(f * part, part)
        copies.append(
            pltpu.make_async_copy(orbitals.at[some], out.at[some, :, 0:BX], arrived.at[f])
        )
        copies[-1].start()
    flat.wait()
    for d in range(out.shape[0]):
        for o in range(PAIR):
            for k in range(2):
                out[d, o, BX + k] = rows[4 * o + 2 * k + d % 2]
    for copy in copies:
        copy.wait()


def pack_kernel(got, up, down, mid_pot):
    for dest, first in ((up, SLAB - DEEP), (down, 0)):
        for i in range(DEEP):
            z, xi = divmod(first + i, BX)
            for yi in range(BX):
                dest[i, yi] = gather(got, z, xi, yi)
    odd = iota((8, 128), 0) % 2 == 1
    for yi in range(BX):
        tiles = [[gather(got, z, BX + k, yi) for k in range(2)] for z in range(4)]
        for z in range(4):
            for k in range(2):
                mid_pot[2 * z + k, yi] = tiles[z][k]
        up[DEEP, yi] = jnp.where(odd, tiles[2][1], pltpu.roll(tiles[2][0], 7, 0))
        down[DEEP + 2, yi] = jnp.where(odd, pltpu.roll(tiles[1][1], 1, 0), tiles[1][0])
        for k in range(2):
            up[DEEP + 1 + k, yi] = tiles[3][k]
            down[DEEP + k, yi] = tiles[0][k]


def put(field, row, tiles):
    for yi in range(BX):
        field[row, yi, 0:8] = tiles[yi]
        field[row, yi, 8:16] = tiles[yi]


def take(field, row, yi):
    first = 8 - PAIR if yi < 0 else PAIR if yi >= BX else 0
    return field[row, yi % BX, first : first + 8]


def parts_of(v):
    high = v.astype(jnp.bfloat16)
    rest = v - high.astype(jnp.float32)
    middle = rest.astype(jnp.bfloat16)
    return high, middle, (rest - middle.astype(jnp.float32)).astype(jnp.bfloat16)


def band_parts():
    apart = (iota((128, 128), 0) - iota((128, 128), 1)) % 128
    band = jnp.zeros((128, 128), jnp.float32)
    for j in range(1, REACH + 1):
        band = jnp.where((apart == j) | (apart == 128 - j), coupling[j], band)
    high, middle, low = parts_of(band)
    top = jnp.concatenate([high, middle], axis=1)
    return jnp.concatenate([top, top], axis=0)


def band_product(v, bands):
    high, middle, _ = parts_of(v)
    both = jnp.dot(
        jnp.concatenate([high, middle], axis=1), bands, preferred_element_type=jnp.float32
    )
    return both[:, :128] + both[:, 128:]


def sweep(field, far_z, bands, first, last, count, one):
    def chunk(c, carry):
        start = first + c * count
        along_z(field, far_z, bands, start + REACH, start, count)
        for r in range(0, count, 2):
            one(start + r)
        return carry

    lax.fori_loop(0, (last - first) // count, chunk, 0)


def along_z(field, far_z, bands, row, i, count):
    v = field[pl.ds(row, count), :, 0:8].reshape(count * BX * 8, 128)
    far_z[pl.ds(i, count)] = band_product(v, bands).reshape(count, BX, 8, 128)


def apply(field, pot, far_z, row, pot_row, i):
    totals = [[], []]
    for begin in range(0, BX, 4):
        lines = [
            [take(field, row + r, y) for y in range(begin - REACH, begin + 4 + REACH)]
            for r in range(2)
        ]
        for yi in range(begin, begin + 4):
            e = REACH + yi - begin
            x = {0: lines[0][e], 1: lines[1][e]}
            for d in (*range(-REACH, 0), *range(2, REACH + 2)):
                x[d] = take(field, row + d, yi)
            for r in range(2):
                line = lines[r]
                total = pot[pot_row + r, yi] * line[e] + far_z[i + r, yi]
                for j in range(1, REACH + 1):
                    near = (x[r + j] + x[r - j]) + (line[e + j] + line[e - j])
                    total = total + coupling[j] * near
                totals[r].append(total)
    return totals


WHOLE = tuple((8 * z + 2 * k, 8 * z + 2 * k + 4) for z in range(4) for k in range(2))


def put_pots(pot, mine, sources, slots, row):
    odd = iota((8, 128), 0) % 2 == 1
    for slot, (even_row, odd_row) in enumerate(slots):
        for source, parity in zip(sources, (mine, 1 - mine)):
            for yi in range(BX):
                tile = diagonal + source[slot, yi] * (1.0 / half_width)
                pot[row + even_row + parity, yi] = jnp.where(odd, pltpu.roll(tile, 1, 0), tile)
                pot[row + odd_row + parity, yi] = jnp.where(odd, tile, pltpu.roll(tile, 7, 0))


def steps(field0, field1, field2, pot, far_z):
    def first(i):
        for r, ts in enumerate(apply(field0, pot, far_z, i + REACH, i, i)):
            put(field1, i + r, ts)

    def second(i):
        for r, ts in enumerate(apply(field1, pot, far_z, i + REACH, i + REACH, i)):
            before = i + r + FLAT
            put(field2, i + r, [t + t - take(field0, before, yi) for yi, t in enumerate(ts)])

    return first, second


def inner_kernel(core, got, mid_pot, far_mid, field0, field1, field2, pot, far_z):
    bands = band_parts()
    for z in range(4):
        def fill(xi, carry, z=z):
            put(field0, DEEP + z * BX + xi, [gather(got, z, xi, yi) for yi in range(BX)])
            return carry

        lax.fori_loop(0, BX, fill, 0)
    put_pots(pot, core[0], (mid_pot, far_mid), WHOLE, FLAT)
    first, second = steps(field0, field1, field2, pot, far_z)
    sweep(field0, far_z, bands, *IN1, IN1[1] - IN1[0], first)
    sweep(field1, far_z, bands, *IN2, IN2[1] - IN2[0], second)


def pots_kernel(low, high, low_pot, high_pot):
    low_pot[...] = low[DEEP:]
    high_pot[...] = high[DEEP:]


def edge_kernel(low, high, _, field0, far_z):
    bands = band_parts()

    def edge(i, carry):
        put(field0, i, [low[i, yi] for yi in range(BX)])
        put(field0, DEEP + SLAB + i, [high[i, yi] for yi in range(BX)])
        return carry

    lax.fori_loop(0, DEEP, edge, 0)
    along_z(field0, far_z, bands, REACH, 0, IN1[0])
    along_z(field0, far_z, bands, REACH + IN1[1], IN1[1], SLAB + 2 * FLAT - IN1[1])


def outer_kernel(
    core, low_pot, high_pot, far_low, far_high, field0, _1, _2, _3, _4,
    out, field1, field2, pot, far_z,
):
    bands = band_parts()
    mine = core[0]
    put_pots(pot, mine, (low_pot, far_low), ((0, 2), (4, 8), (6, 10)), 0)
    put_pots(pot, mine, (high_pot, far_high), ((0, 4), (2, 6), (8, 10)), FLAT + SLAB)
    first, second = steps(field0, field1, field2, pot, far_z)

    def third(i):
        for r, ts in enumerate(apply(field2, pot, far_z, i + REACH, i + FLAT, i)):
            for yi, t in enumerate(ts):
                start = ((i // BX) * 4 * PAIR * BX + i % BX + r) * BX + yi
                out[pl.ds(start, 8, stride=BX * BX), :] = (
                    t + t - take(field1, i + r + FLAT, yi)
                )

    ends1, ends2, half = SLAB + 2 * FLAT, SLAB + FLAT, SLAB // 2

    def rows(one, begin, end):
        for r in range(begin, end, 2):
            one(r)

    def ahead(field, begin, end):
        along_z(field, far_z, bands, begin + REACH, begin, end - begin)

    rows(first, 0, IN1[0])
    rows(first, IN1[1], ends1), ahead(field1, 0, IN2[0])
    rows(second, 0, IN2[0]), ahead(field1, IN2[1], ends2)
    rows(second, IN2[1], ends2), ahead(field2, 0, half)
    rows(third, 0, half), ahead(field2, half, SLAB)
    rows(third, half, SLAB)


def iota(shape, dim):
    return lax.broadcasted_iota(jnp.int32, shape, dim)


def spread(orbital_count):
    shape = (orbital_count * BX, orbital_count)
    return (iota(shape, 0) // BX == iota(shape, 1)).astype(jnp.float32)


def same_y(orbital_count):
    shape = (orbital_count * BX, orbital_count * BX)
    return iota(shape, 0) % BX == iota(shape, 1) % BX


def dot(a, b, dims=((1,), (0,))):
    return lax.dot_general(
        a, b, (dims, ((), ())), precision=highest, preferred_element_type=jnp.float32
    )


def pair_of_rows(y, x):
    rows = y.shape[0] * BX
    return jnp.concatenate([y[:, x].reshape(rows, 128), y[:, x + 1].reshape(rows, 128)], axis=1)


def across(a, b):
    return lax.dot_general(a, b, (((1,), (1,)), ((), ())), preferred_element_type=jnp.float32)


def gram_kernel(scale, y, out):
    n = y.shape[0]
    total = None
    for x in range(0, BX, 2):
        high, middle, low = parts_of(pair_of_rows(y, x))
        part = 0.5 * (across(high, high) + across(middle, middle))
        part = part + (across(high, middle) + across(high, low))
        total = part if total is None else total + part
    total = jnp.where(same_y(n), total, 0.0) * scale
    ones = spread(n)
    gram = dot(dot(ones, total, ((0,), (0,))), ones)
    gram = gram + gram.T
    half = n // 2
    upper = iota((half, half), 0) <= iota((half, half), 1)
    kept = jnp.concatenate(
        [jnp.where(upper, gram[:half, :half], gram[half:, half:]), gram[:half, half:]], axis=1
    )
    unit = iota((half, half), 0) == iota((half, half), 1)
    ends = jnp.sum(jnp.where(unit, gram[half:, half:], 0.0), axis=0, keepdims=True)
    ends = jnp.concatenate([ends, jnp.zeros((1, 128 - half), jnp.float32)], axis=1)
    rows = jnp.concatenate([kept[4 * k : 4 * k + 4] for k in range(4)], axis=1)
    rows = jnp.concatenate([rows, ends], axis=0)
    for d in range(out.shape[0] // 5):
        out[5 * d : 5 * d + 5] = rows


def finish_kernel(parts, y2, out, factor):
    n = factor.shape[0]
    half = n // 2
    rows = []
    for r in range(5):
        total = None
        for d in range(0, parts.shape[0] // 5, 8):
            tile = parts[pl.ds(5 * d + r, 8, stride=5), :]
            total = tile if total is None else total + tile
        rows.append(jnp.sum(total, axis=0, keepdims=True))
    rows = jnp.concatenate(rows, axis=0)
    kept = jnp.concatenate([rows[:4, n * k : n * k + n] for k in range(4)], axis=0)
    across = kept[:, half:]
    unit = iota((half, half), 0) == iota((half, half), 1)
    upper = iota((half, half), 0) < iota((half, half), 1)
    mixed = kept[:, :half]
    turned = mixed.T
    first = jnp.where(upper | unit, mixed, turned)
    last = jnp.where(upper, turned, mixed)
    last = jnp.where(unit, jnp.broadcast_to(rows[4:5, :half], (half, half)), last)
    gram = jnp.concatenate(
        [jnp.concatenate([first, across], axis=1), jnp.concatenate([across.T, last], axis=1)],
        axis=0,
    )
    unit = (iota((n, n), 0) == iota((n, n), 1)).astype(jnp.float32)
    left = jnp.concatenate([gram, unit, jnp.zeros((n, 128 - 2 * n), jnp.float32)], axis=1)
    row_of = iota((n, 128), 0)
    finished = []
    for k in range(0, n, STEP):
        entry = {
            (i, j): jnp.broadcast_to(left[k + i : k + i + 1, k + j : k + j + 1], (1, 128))
            for i in range(STEP)
            for j in range(i + 1)
        }
        columns = [
            jnp.broadcast_to(left[:, k + j : k + j + 1], (n, 128)) for j in range(STEP)
        ]
        lines = [left[k + j : k + j + 1] for j in range(STEP)]
        for j in range(STEP):
            inverse = lax.rsqrt(entry[j, j])
            lines[j] = lines[j] * inverse
            columns[j] = columns[j] * inverse
            for i in range(j + 1, STEP):
                entry[i, j] = entry[i, j] * inverse
            for i in range(j + 1, STEP):
                for m in range(j + 1, i + 1):
                    entry[i, m] = entry[i, m] - entry[i, j] * entry[m, j]
                lines[i] = lines[i] - entry[i, j] * lines[j]
                columns[i] = columns[i] - entry[i, j] * columns[j]
        finished += lines
        change = None
        for line, column in zip(lines, columns):
            part = column * line
            change = part if change is None else change + part
        left = jnp.where(row_of >= k + STEP, left - change, left)
    done = jnp.concatenate(finished, axis=0)
    factor[...] = jnp.where(iota((n, n), 0) <= iota((n, n), 1), done[:, :n], 0.0)
    mixer = done[:, n : 2 * n]
    m_high, m_middle, m_low = parts_of(mixer)
    wide = jnp.concatenate([m_high, m_high, m_high, m_middle, m_middle, m_low], axis=1)
    wide = jnp.concatenate([wide, jnp.zeros((n, 256 - 6 * n), jnp.bfloat16)], axis=1)
    for xy in range(0, BX * BX, 2):
        both = []
        for r in range(2):
            both.append(jnp.concatenate([y2[pl.ds(xy + r + 512 * k, 8, stride=64), :] for k in range(n // 8)], axis=0))
        v = jnp.concatenate(both, axis=1)
        high, middle, low = parts_of(v)
        stack = jnp.concatenate([high, middle, low, high, middle, high, jnp.zeros((256 - 6 * n, 256), jnp.bfloat16)], axis=0)
        mixed = jnp.dot(wide, stack, preferred_element_type=jnp.float32)
        for r in range(2):
            for k in range(n // 8):
                out[pl.ds(xy + r + 512 * k, 8, stride=64), :] = mixed[8 * k : 8 * k + 8, 128 * r : 128 * r + 128]


def call(kernel, out_shape, in_specs, scratch=(), limit=8, flops=0, moved=0, aliases={}):
    return pl.pallas_call(
        kernel,
        out_shape=out_shape,
        in_specs=in_specs,
        out_specs=jax.tree.map(lambda _: VMEM, out_shape),
        scratch_shapes=list(scratch),
        input_output_aliases=aliases,
        compiler_params=pltpu.CompilerParams(vmem_limit_bytes=limit << 20),
        cost_estimate=pl.CostEstimate(flops=flops, bytes_accessed=moved, transcendentals=0),
    )


def f32(*shape):
    return jax.ShapeDtypeStruct(shape, jnp.float32)


def per_device(orbitals, potential):
    n = orbitals.shape[0]
    slabs = lax.axis_size("s")
    group = lax.axis_size("z") * lax.axis_size("gy")
    core = lax.axis_index("gy") & 1
    away = pl.BlockSpec(memory_space=pltpu.HBM)
    sent = call(
        message_kernel,
        f32(group, PAIR, BLOCK, BX, 128),
        [away, away],
        [pltpu.VMEM((BX, BX, 128), jnp.float32), pltpu.SemaphoreType.DMA((FLOWS + 1,))],
    )(
        pltpu.with_memory_space_constraint(orbitals.reshape(group, PAIR, BX, BX, 128), pltpu.HBM),
        pltpu.with_memory_space_constraint(potential, pltpu.HBM),
    )
    got = lax.all_to_all(sent, ("z", "gy"), 0, 0, tiled=True)
    got = got.reshape(group * PAIR * BLOCK * BX, 128)
    up, down, mid_pot = call(
        pack_kernel, (f32(DEEP + 3, 8, 8, 128),) * 2 + (f32(8, 8, 8, 128),), [VMEM]
    )(got)
    ring = [(i, (i + 1) % slabs) for i in range(slabs)]
    back_ring = [(j, i) for i, j in ring]
    twin = [(i, i ^ 1) for i in range(lax.axis_size("gy"))]
    low = lax.ppermute(up, "s", ring)
    high = lax.ppermute(down, "s", back_ring)
    far_mid = lax.ppermute(mid_pot, "gy", twin)
    own = (core.reshape(1),)
    fields = tuple(f32(rows, BX, 16, 128) for rows in (SLAB + 2 * DEEP, SLAB + 2 * FLAT, SLAB + FLAT))
    fields += (f32(SLAB + 2 * FLAT, BX, 8, 128),)
    far_z = [pltpu.VMEM((SLAB + 2 * FLAT, BX, 8, 128), jnp.float32)]
    inner = call(inner_kernel, fields, [SMEM] + [VMEM] * 3, far_z, 10, flops=1 << 32)(
        *own, got, mid_pot, far_mid
    )
    low, high, inner = lax.optimization_barrier((low, high, inner))
    low_pot, high_pot = call(pots_kernel, (f32(3, 8, 8, 128),) * 2, [VMEM] * 2)(low, high)
    far_low = lax.ppermute(low_pot, "gy", twin)
    far_high = lax.ppermute(high_pot, "gy", twin)
    field0, field1, field2, pot = inner
    field0, products = call(
        edge_kernel, (fields[0], fields[3]), [VMEM] * 3, (), 10, flops=1 << 30, aliases={2: 0}
    )(low, high, field0)
    filtered = call(
        outer_kernel,
        (f32(group * PAIR * BX * BX, 128),) + fields[1:] + (fields[3],),
        [SMEM] + [VMEM] * 9,
        (),
        10,
        aliases={6 + k: 1 + k for k in range(4)},
    )(*own, low_pot, high_pot, far_low, far_high, field0, field1, field2, pot, products)[0]
    filtered = filtered.reshape(group, PAIR, BX, BX, 128)
    back = lax.all_to_all(filtered, ("z", "gy"), 0, 0, tiled=True).reshape(n, BX, BX, 128)
    devices = slabs * group
    cells = float(devices * BX * BX * 128)
    parts = call(
        functools.partial(gram_kernel, 1.0 / cells), f32(devices * 5, 128), [VMEM]
    )(back)
    parts = lax.all_to_all(
        parts.reshape(devices, 1, 5 * 128), ("gy", "z", "s"), 0, 0, tiled=True
    ).reshape(devices * 5, 128)
    made, factor = call(finish_kernel, (f32(n * BX * BX, 128), f32(n, n)), [VMEM, VMEM])(
        parts, back.reshape(n * BX * BX, 128)
    )
    return made.reshape(n, BX, BX, 128), factor


def solution(mesh):
    shape = mesh.devices.shape
    fine = Mesh(mesh.devices.reshape(shape[0] // 4, 4, shape[1]), ("s", "z", "gy"))
    return jax.shard_map(
        per_device,
        mesh=fine,
        in_specs=(P(None, ("s", "z"), "gy", None), P(("s", "z"), "gy", None)),
        out_specs=(P(None, ("s", "z"), "gy", None), P()),
        check_vma=False,
    )
```

```python
import functools

import jax
import jax.numpy as jnp
from jax import lax
from jax.experimental import pallas as pl
from jax.experimental.pallas import tpu as pltpu
from jax.sharding import Mesh
from jax.sharding import PartitionSpec as P

stencil_weights = (
    -5369.0 / 1800.0,
    12.0 / 7.0,
    -15.0 / 56.0,
    10.0 / 189.0,
    -1.0 / 112.0,
    2.0 / 1925.0,
    -1.0 / 16632.0,
)
grid_spacing = 0.5
filter_low = 4.0
filter_high = 46.0
centre_shift = 0.5 * (filter_high + filter_low)
half_width = 0.5 * (filter_high - filter_low)
kinetic = -0.5 / grid_spacing**2
diagonal = (kinetic * 3.0 * stencil_weights[0] - centre_shift) / half_width
coupling = tuple(kinetic * w / half_width for w in stencil_weights)
highest = lax.Precision.HIGHEST

REACH = 6
DEEP = 3 * REACH
FLAT = 2 * REACH
FLOWS = 4
STEP = 8
PAIR = 2
IN1 = (DEEP, DEEP + 20)
OWN = range(DEEP, DEEP + 32)
BEGUN = (DEEP - REACH, DEEP + 20)
IN2 = (DEEP, DEEP + 8)
BX = 8
BLOCK = BX + 2
SLAB = 4 * BX
VMEM = pl.BlockSpec(memory_space=pltpu.VMEM)
SMEM = pl.BlockSpec(memory_space=pltpu.SMEM)


def gather(got, z, xi, yi):
    return got[pl.ds(((z * 4) * PAIR * BLOCK + xi) * BX + yi, 8, stride=BLOCK * BX), :]


def message_kernel(orbitals, potential, out, rows, arrived):
    flat = pltpu.make_async_copy(potential, rows, arrived.at[FLOWS])
    flat.start()
    part = out.shape[0] // FLOWS
    copies = []
    for f in range(FLOWS):
        some = pl.ds(f * part, part)
        copies.append(
            pltpu.make_async_copy(orbitals.at[some], out.at[some, :, 0:BX], arrived.at[f])
        )
        copies[-1].start()
    flat.wait()
    for d in range(out.shape[0]):
        for o in range(PAIR):
            for k in range(2):
                out[d, o, BX + k] = rows[4 * o + 2 * k + d % 2]
    for copy in copies:
        copy.wait()


def pack_kernel(got, up, down, mid_pot):
    for dest, first in ((up, SLAB - DEEP), (down, 0)):
        for i in range(DEEP):
            z, xi = divmod(first + i, BX)
            for yi in range(BX):
                dest[i, yi] = gather(got, z, xi, yi)
    odd = iota((8, 128), 0) % 2 == 1
    for yi in range(BX):
        tiles = [[gather(got, z, BX + k, yi) for k in range(2)] for z in range(4)]
        for z in range(4):
            for k in range(2):
                mid_pot[2 * z + k, yi] = tiles[z][k]
        up[DEEP, yi] = jnp.where(odd, tiles[2][1], pltpu.roll(tiles[2][0], 7, 0))
        down[DEEP + 2, yi] = jnp.where(odd, pltpu.roll(tiles[1][1], 1, 0), tiles[1][0])
        for k in range(2):
            up[DEEP + 1 + k, yi] = tiles[3][k]
            down[DEEP + k, yi] = tiles[0][k]


def put(field, row, tiles):
    for yi in range(BX):
        field[row, yi, 0:8] = tiles[yi]
        field[row, yi, 8:16] = tiles[yi]


def take(field, row, yi):
    first = 8 - PAIR if yi < 0 else PAIR if yi >= BX else 0
    return field[row, yi % BX, first : first + 8]


def parts_of(v):
    high = v.astype(jnp.bfloat16)
    rest = v - high.astype(jnp.float32)
    middle = rest.astype(jnp.bfloat16)
    return high, middle, (rest - middle.astype(jnp.float32)).astype(jnp.bfloat16)


def band_parts():
    apart = (iota((128, 128), 0) - iota((128, 128), 1)) % 128
    band = jnp.zeros((128, 128), jnp.float32)
    for j in range(1, REACH + 1):
        band = jnp.where((apart == j) | (apart == 128 - j), coupling[j], band)
    high, middle, low = parts_of(band)
    top = jnp.concatenate([high, middle], axis=1)
    return jnp.concatenate([top, top], axis=0)


def band_product(v, bands):
    high, middle, _ = parts_of(v)
    both = jnp.dot(
        jnp.concatenate([high, middle], axis=1), bands, preferred_element_type=jnp.float32
    )
    return both[:, :128] + both[:, 128:]


def sweep(field, far_z, bands, first, last, count, one):
    def chunk(c, carry):
        start = first + c * count
        along_z(field, far_z, bands, start + REACH, start, count)
        for r in range(0, count, 2):
            one(start + r)
        return carry

    lax.fori_loop(0, (last - first) // count, chunk, 0)


def along_z(field, far_z, bands, row, i, count):
    v = field[pl.ds(row, count), :, 0:8].reshape(count * BX * 8, 128)
    far_z[pl.ds(i, count)] = band_product(v, bands).reshape(count, BX, 8, 128)


def apply(field, pot, far_z, row, pot_row, i, known=None):
    totals = [[], []]
    for begin in range(0, BX, 4):
        lines = [
            [take(field, row + r, y) for y in range(begin - REACH, begin + 4 + REACH)]
            for r in range(2)
        ]
        for yi in range(begin, begin + 4):
            e = REACH + yi - begin
            x = {0: lines[0][e], 1: lines[1][e]}
            for d in (*range(-REACH, 0), *range(2, REACH + 2)):
                if known is None or row + d in known:
                    x[d] = take(field, row + d, yi)
            for r in range(2):
                line = lines[r]
                total = pot[pot_row + r, yi] * line[e] + far_z[i + r, yi]
                for j in range(1, REACH + 1):
                    near = line[e + j] + line[e - j]
                    beside = [x[d] for d in (r + j, r - j) if d in x]
                    if beside:
                        near = sum(beside[1:], beside[0]) + near
                    total = total + coupling[j] * near
                totals[r].append(total)
    return totals


WHOLE = tuple((8 * z + 2 * k, 8 * z + 2 * k + 4) for z in range(4) for k in range(2))


def put_pots(pot, mine, sources, slots, row):
    odd = iota((8, 128), 0) % 2 == 1
    for slot, (even_row, odd_row) in enumerate(slots):
        for source, parity in zip(sources, (mine, 1 - mine)):
            for yi in range(BX):
                tile = diagonal + source[slot, yi] * (1.0 / half_width)
                pot[row + even_row + parity, yi] = jnp.where(odd, pltpu.roll(tile, 1, 0), tile)
                pot[row + odd_row + parity, yi] = jnp.where(odd, tile, pltpu.roll(tile, 7, 0))


def steps(field0, field1, field2, pot, far_z):
    def first(i):
        for r, ts in enumerate(apply(field0, pot, far_z, i + REACH, i, i)):
            put(field1, i + r, ts)

    def second(i):
        for r, ts in enumerate(apply(field1, pot, far_z, i + REACH, i + REACH, i)):
            before = i + r + FLAT
            put(field2, i + r, [t + t - take(field0, before, yi) for yi, t in enumerate(ts)])

    return first, second


def inner_kernel(core, got, mid_pot, far_mid, field0, field1, field2, pot, begun, far_z):
    bands = band_parts()
    for z in range(4):
        def fill(xi, carry, z=z):
            put(field0, DEEP + z * BX + xi, [gather(got, z, xi, yi) for yi in range(BX)])
            return carry

        lax.fori_loop(0, BX, fill, 0)
    put_pots(pot, core[0], (mid_pot, far_mid), WHOLE, FLAT)
    first, second = steps(field0, field1, field2, pot, far_z)
    sweep(field0, far_z, bands, *IN1, IN1[1] - IN1[0], first)
    sweep(field1, far_z, bands, *IN2, IN2[1] - IN2[0], second)
    for at, start in enumerate(BEGUN):
        along_z(field0, far_z, bands, start + REACH, start, REACH)
        for r in range(0, REACH, 2):
            i = start + r
            totals = apply(field0, pot, far_z, i + REACH, i, i, OWN)
            for k in range(2):
                for yi in range(BX):
                    begun[at * REACH + r + k, yi] = totals[k][yi]


def pots_kernel(low, high, low_pot, high_pot):
    low_pot[...] = low[DEEP:]
    high_pot[...] = high[DEEP:]


def edge_kernel(low, high, _, field0, far_z):
    bands = band_parts()

    def edge(i, carry):
        put(field0, i, [low[i, yi] for yi in range(BX)])
        put(field0, DEEP + SLAB + i, [high[i, yi] for yi in range(BX)])
        return carry

    lax.fori_loop(0, DEEP, edge, 0)
    along_z(field0, far_z, bands, REACH, 0, FLAT)
    along_z(field0, far_z, bands, REACH + FLAT + SLAB, FLAT + SLAB, FLAT)


def outer_kernel(
    core, low_pot, high_pot, far_low, far_high, field0, begun, _1, _2, _3, _4,
    out, field1, field2, pot, far_z,
):
    bands = band_parts()
    mine = core[0]
    put_pots(pot, mine, (low_pot, far_low), ((0, 2), (4, 8), (6, 10)), 0)
    put_pots(pot, mine, (high_pot, far_high), ((0, 4), (2, 6), (8, 10)), FLAT + SLAB)
    first, second = steps(field0, field1, field2, pot, far_z)

    def third(i):
        for r, ts in enumerate(apply(field2, pot, far_z, i + REACH, i + FLAT, i)):
            for yi, t in enumerate(ts):
                start = ((i // BX) * 4 * PAIR * BX + i % BX + r) * BX + yi
                out[pl.ds(start, 8, stride=BX * BX), :] = (
                    t + t - take(field1, i + r + FLAT, yi)
                )

    ends1, ends2, half = SLAB + 2 * FLAT, SLAB + FLAT, SLAB // 2

    def rows(one, begin, end):
        for r in range(begin, end, 2):
            one(r)

    def ahead(field, begin, end):
        along_z(field, far_z, bands, begin + REACH, begin, end - begin)

    def complete(at):
        for r in range(REACH):
            i = BEGUN[at] + r
            tiles = []
            for yi in range(BX):
                total = begun[at * REACH + r, yi]
                for j in range(1, REACH + 1):
                    for row in (i + REACH - j, i + REACH + j):
                        if row not in OWN:
                            total = total + coupling[j] * take(field0, row, yi)
                tiles.append(total)
            put(field1, i, tiles)

    rows(first, 0, FLAT), complete(0)
    complete(1), rows(first, FLAT + SLAB, ends1), ahead(field1, 0, IN2[0])
    rows(second, 0, IN2[0]), ahead(field1, IN2[1], ends2)
    rows(second, IN2[1], ends2), ahead(field2, 0, half)
    rows(third, 0, half), ahead(field2, half, SLAB)
    rows(third, half, SLAB)


def iota(shape, dim):
    return lax.broadcasted_iota(jnp.int32, shape, dim)


def spread(orbital_count):
    shape = (orbital_count * BX, orbital_count)
    return (iota(shape, 0) // BX == iota(shape, 1)).astype(jnp.float32)


def same_y(orbital_count):
    shape = (orbital_count * BX, orbital_count * BX)
    return iota(shape, 0) % BX == iota(shape, 1) % BX


def dot(a, b, dims=((1,), (0,))):
    return lax.dot_general(
        a, b, (dims, ((), ())), precision=highest, preferred_element_type=jnp.float32
    )


def pair_of_rows(y, x):
    rows = y.shape[0] * BX
    return jnp.concatenate([y[:, x].reshape(rows, 128), y[:, x + 1].reshape(rows, 128)], axis=1)


def across(a, b):
    return lax.dot_general(a, b, (((1,), (1,)), ((), ())), preferred_element_type=jnp.float32)


def gram_kernel(scale, y, out):
    n = y.shape[0]
    total = None
    for x in range(0, BX, 2):
        high, middle, low = parts_of(pair_of_rows(y, x))
        part = 0.5 * (across(high, high) + across(middle, middle))
        part = part + (across(high, middle) + across(high, low))
        total = part if total is None else total + part
    total = jnp.where(same_y(n), total, 0.0) * scale
    ones = spread(n)
    gram = dot(dot(ones, total, ((0,), (0,))), ones)
    gram = gram + gram.T
    half = n // 2
    upper = iota((half, half), 0) <= iota((half, half), 1)
    kept = jnp.concatenate(
        [jnp.where(upper, gram[:half, :half], gram[half:, half:]), gram[:half, half:]], axis=1
    )
    unit = iota((half, half), 0) == iota((half, half), 1)
    ends = jnp.sum(jnp.where(unit, gram[half:, half:], 0.0), axis=0, keepdims=True)
    ends = jnp.concatenate([ends, jnp.zeros((1, 128 - half), jnp.float32)], axis=1)
    rows = jnp.concatenate([kept[4 * k : 4 * k + 4] for k in range(4)], axis=1)
    rows = jnp.concatenate([rows, ends], axis=0)
    for d in range(out.shape[0] // 5):
        out[5 * d : 5 * d + 5] = rows


def finish_kernel(parts, y2, out, factor):
    n = factor.shape[0]
    half = n // 2
    rows = []
    for r in range(5):
        total = None
        for d in range(0, parts.shape[0] // 5, 8):
            tile = parts[pl.ds(5 * d + r, 8, stride=5), :]
            total = tile if total is None else total + tile
        rows.append(jnp.sum(total, axis=0, keepdims=True))
    rows = jnp.concatenate(rows, axis=0)
    kept = jnp.concatenate([rows[:4, n * k : n * k + n] for k in range(4)], axis=0)
    across = kept[:, half:]
    unit = iota((half, half), 0) == iota((half, half), 1)
    upper = iota((half, half), 0) < iota((half, half), 1)
    mixed = kept[:, :half]
    turned = mixed.T
    first = jnp.where(upper | unit, mixed, turned)
    last = jnp.where(upper, turned, mixed)
    last = jnp.where(unit, jnp.broadcast_to(rows[4:5, :half], (half, half)), last)
    gram = jnp.concatenate(
        [jnp.concatenate([first, across], axis=1), jnp.concatenate([across.T, last], axis=1)],
        axis=0,
    )
    unit = (iota((n, n), 0) == iota((n, n), 1)).astype(jnp.float32)
    left = jnp.concatenate([gram, unit, jnp.zeros((n, 128 - 2 * n), jnp.float32)], axis=1)
    row_of = iota((n, 128), 0)
    finished = []
    for k in range(0, n, STEP):
        entry = {
            (i, j): jnp.broadcast_to(left[k + i : k + i + 1, k + j : k + j + 1], (1, 128))
            for i in range(STEP)
            for j in range(i + 1)
        }
        columns = [
            jnp.broadcast_to(left[:, k + j : k + j + 1], (n, 128)) for j in range(STEP)
        ]
        lines = [left[k + j : k + j + 1] for j in range(STEP)]
        for j in range(STEP):
            inverse = lax.rsqrt(entry[j, j])
            lines[j] = lines[j] * inverse
            columns[j] = columns[j] * inverse
            for i in range(j + 1, STEP):
                entry[i, j] = entry[i, j] * inverse
            for i in range(j + 1, STEP):
                for m in range(j + 1, i + 1):
                    entry[i, m] = entry[i, m] - entry[i, j] * entry[m, j]
                lines[i] = lines[i] - entry[i, j] * lines[j]
                columns[i] = columns[i] - entry[i, j] * columns[j]
        finished += lines
        change = None
        for line, column in zip(lines, columns):
            part = column * line
            change = part if change is None else change + part
        left = jnp.where(row_of >= k + STEP, left - change, left)
    done = jnp.concatenate(finished, axis=0)
    factor[...] = jnp.where(iota((n, n), 0) <= iota((n, n), 1), done[:, :n], 0.0)
    mixer = done[:, n : 2 * n]
    m_high, m_middle, m_low = parts_of(mixer)
    wide = jnp.concatenate([m_high, m_high, m_high, m_middle, m_middle, m_low], axis=1)
    wide = jnp.concatenate([wide, jnp.zeros((n, 256 - 6 * n), jnp.bfloat16)], axis=1)
    for xy in range(0, BX * BX, 2):
        both = []
        for r in range(2):
            both.append(jnp.concatenate([y2[pl.ds(xy + r + 512 * k, 8, stride=64), :] for k in range(n // 8)], axis=0))
        v = jnp.concatenate(both, axis=1)
        high, middle, low = parts_of(v)
        stack = jnp.concatenate([high, middle, low, high, middle, high, jnp.zeros((256 - 6 * n, 256), jnp.bfloat16)], axis=0)
        mixed = jnp.dot(wide, stack, preferred_element_type=jnp.float32)
        for r in range(2):
            for k in range(n // 8):
                out[pl.ds(xy + r + 512 * k, 8, stride=64), :] = mixed[8 * k : 8 * k + 8, 128 * r : 128 * r + 128]


def call(kernel, out_shape, in_specs, scratch=(), limit=8, flops=0, moved=0, aliases={}):
    return pl.pallas_call(
        kernel,
        out_shape=out_shape,
        in_specs=in_specs,
        out_specs=jax.tree.map(lambda _: VMEM, out_shape),
        scratch_shapes=list(scratch),
        input_output_aliases=aliases,
        compiler_params=pltpu.CompilerParams(vmem_limit_bytes=limit << 20),
        cost_estimate=pl.CostEstimate(flops=flops, bytes_accessed=moved, transcendentals=0),
    )


def f32(*shape):
    return jax.ShapeDtypeStruct(shape, jnp.float32)


def per_device(orbitals, potential):
    n = orbitals.shape[0]
    slabs = lax.axis_size("s")
    group = lax.axis_size("z") * lax.axis_size("gy")
    core = lax.axis_index("gy") & 1
    away = pl.BlockSpec(memory_space=pltpu.HBM)
    sent = call(
        message_kernel,
        f32(group, PAIR, BLOCK, BX, 128),
        [away, away],
        [pltpu.VMEM((BX, BX, 128), jnp.float32), pltpu.SemaphoreType.DMA((FLOWS + 1,))],
    )(
        pltpu.with_memory_space_constraint(orbitals.reshape(group, PAIR, BX, BX, 128), pltpu.HBM),
        pltpu.with_memory_space_constraint(potential, pltpu.HBM),
    )
    got = lax.all_to_all(sent, ("z", "gy"), 0, 0, tiled=True)
    got = got.reshape(group * PAIR * BLOCK * BX, 128)
    up, down, mid_pot = call(
        pack_kernel, (f32(DEEP + 3, 8, 8, 128),) * 2 + (f32(8, 8, 8, 128),), [VMEM]
    )(got)
    ring = [(i, (i + 1) % slabs) for i in range(slabs)]
    back_ring = [(j, i) for i, j in ring]
    twin = [(i, i ^ 1) for i in range(lax.axis_size("gy"))]
    low = lax.ppermute(up, "s", ring)
    high = lax.ppermute(down, "s", back_ring)
    far_mid = lax.ppermute(mid_pot, "gy", twin)
    own = (core.reshape(1),)
    fields = tuple(f32(rows, BX, 16, 128) for rows in (SLAB + 2 * DEEP, SLAB + 2 * FLAT, SLAB + FLAT))
    fields += (f32(SLAB + 2 * FLAT, BX, 8, 128),)
    far_z = [pltpu.VMEM((SLAB + 2 * FLAT, BX, 8, 128), jnp.float32)]
    inner = call(inner_kernel, fields + (f32(2 * REACH, BX, 8, 128),), [SMEM] + [VMEM] * 3, far_z, 10, flops=1 << 32)(
        *own, got, mid_pot, far_mid
    )
    low, high, inner = lax.optimization_barrier((low, high, inner))
    low_pot, high_pot = call(pots_kernel, (f32(3, 8, 8, 128),) * 2, [VMEM] * 2)(low, high)
    far_low = lax.ppermute(low_pot, "gy", twin)
    far_high = lax.ppermute(high_pot, "gy", twin)
    field0, field1, field2, pot, begun = inner
    field0, products = call(
        edge_kernel, (fields[0], fields[3]), [VMEM] * 3, (), 10, flops=1 << 30, aliases={2: 0}
    )(low, high, field0)
    filtered = call(
        outer_kernel,
        (f32(group * PAIR * BX * BX, 128),) + fields[1:] + (fields[3],),
        [SMEM] + [VMEM] * 10,
        (),
        10,
        aliases={7 + k: 1 + k for k in range(4)},
    )(*own, low_pot, high_pot, far_low, far_high, field0, begun, field1, field2, pot, products)[0]
    filtered = filtered.reshape(group, PAIR, BX, BX, 128)
    back = lax.all_to_all(filtered, ("z", "gy"), 0, 0, tiled=True).reshape(n, BX, BX, 128)
    devices = slabs * group
    cells = float(devices * BX * BX * 128)
    parts = call(
        functools.partial(gram_kernel, 1.0 / cells), f32(devices * 5, 128), [VMEM]
    )(back)
    parts = lax.all_to_all(
        parts.reshape(devices, 1, 5 * 128), ("gy", "z", "s"), 0, 0, tiled=True
    ).reshape(devices * 5, 128)
    made, factor = call(finish_kernel, (f32(n * BX * BX, 128), f32(n, n)), [VMEM, VMEM])(
        parts, back.reshape(n * BX * BX, 128)
    )
    return made.reshape(n, BX, BX, 128), factor


def solution(mesh):
    shape = mesh.devices.shape
    fine = Mesh(mesh.devices.reshape(shape[0] // 4, 4, shape[1]), ("s", "z", "gy"))
    return jax.shard_map(
        per_device,
        mesh=fine,
        in_specs=(P(None, ("s", "z"), "gy", None), P(("s", "z"), "gy", None)),
        out_specs=(P(None, ("s", "z"), "gy", None), P()),
        check_vma=False,
    )
```

```python
import functools

import jax
import jax.numpy as jnp
from jax import lax
from jax.experimental import pallas as pl
from jax.experimental.pallas import tpu as pltpu
from jax.sharding import Mesh
from jax.sharding import PartitionSpec as P

stencil_weights = (
    -5369.0 / 1800.0,
    12.0 / 7.0,
    -15.0 / 56.0,
    10.0 / 189.0,
    -1.0 / 112.0,
    2.0 / 1925.0,
    -1.0 / 16632.0,
)
grid_spacing = 0.5
filter_low = 4.0
filter_high = 46.0
centre_shift = 0.5 * (filter_high + filter_low)
half_width = 0.5 * (filter_high - filter_low)
kinetic = -0.5 / grid_spacing**2
diagonal = (kinetic * 3.0 * stencil_weights[0] - centre_shift) / half_width
coupling = tuple(kinetic * w / half_width for w in stencil_weights)
highest = lax.Precision.HIGHEST

REACH = 6
DEEP = 3 * REACH
FLAT = 2 * REACH
FLOWS = 4
STEP = 8
PAIR = 2
IN1 = (DEEP, DEEP + 20)
OWN = range(DEEP, DEEP + 32)
BEGUN = (DEEP - REACH, DEEP + 20)
IN2 = (DEEP, DEEP + 8)
BX = 8
BLOCK = BX + 2
SLAB = 4 * BX
VMEM = pl.BlockSpec(memory_space=pltpu.VMEM)
SMEM = pl.BlockSpec(memory_space=pltpu.SMEM)


def gather(got, z, xi, yi):
    return got[pl.ds(((z * 4) * PAIR * BLOCK + xi) * BX + yi, 8, stride=BLOCK * BX), :]


def message_kernel(orbitals, potential, out, rows, arrived):
    flat = pltpu.make_async_copy(potential, rows, arrived.at[FLOWS])
    flat.start()
    part = out.shape[0] // FLOWS
    copies = []
    for f in range(FLOWS):
        some = pl.ds(f * part, part)
        copies.append(
            pltpu.make_async_copy(orbitals.at[some], out.at[some, :, 0:BX], arrived.at[f])
        )
        copies[-1].start()
    flat.wait()
    for d in range(out.shape[0]):
        for o in range(PAIR):
            for k in range(2):
                out[d, o, BX + k] = rows[4 * o + 2 * k + d % 2]
    for copy in copies:
        copy.wait()


def pack_kernel(got, up, down, mid_pot):
    for dest, first in ((up, SLAB - DEEP), (down, 0)):
        for i in range(DEEP):
            z, xi = divmod(first + i, BX)
            for yi in range(BX):
                dest[i, yi] = gather(got, z, xi, yi)
    odd = iota((8, 128), 0) % 2 == 1
    for yi in range(BX):
        tiles = [[gather(got, z, BX + k, yi) for k in range(2)] for z in range(4)]
        for z in range(4):
            for k in range(2):
                mid_pot[2 * z + k, yi] = tiles[z][k]
        up[DEEP, yi] = jnp.where(odd, tiles[2][1], pltpu.roll(tiles[2][0], 7, 0))
        down[DEEP + 2, yi] = jnp.where(odd, pltpu.roll(tiles[1][1], 1, 0), tiles[1][0])
        for k in range(2):
            up[DEEP + 1 + k, yi] = tiles[3][k]
            down[DEEP + k, yi] = tiles[0][k]


def put(field, row, tiles):
    for yi in range(BX):
        field[row, yi, 0:8] = tiles[yi]
        field[row, yi, 8:16] = tiles[yi]


def take(field, row, yi):
    first = 8 - PAIR if yi < 0 else PAIR if yi >= BX else 0
    return field[row, yi % BX, first : first + 8]


def parts_of(v):
    high = v.astype(jnp.bfloat16)
    rest = v - high.astype(jnp.float32)
    middle = rest.astype(jnp.bfloat16)
    return high, middle, (rest - middle.astype(jnp.float32)).astype(jnp.bfloat16)


def band_parts():
    apart = (iota((128, 128), 0) - iota((128, 128), 1)) % 128
    band = jnp.zeros((128, 128), jnp.float32)
    for j in range(1, REACH + 1):
        band = jnp.where((apart == j) | (apart == 128 - j), coupling[j], band)
    high, middle, low = parts_of(band)
    top = jnp.concatenate([high, middle], axis=1)
    return jnp.concatenate([top, top], axis=0)


def band_product(v, bands):
    high, middle, _ = parts_of(v)
    both = jnp.dot(
        jnp.concatenate([high, middle], axis=1), bands, preferred_element_type=jnp.float32
    )
    return both[:, :128] + both[:, 128:]


def sweep(field, far_z, bands, first, last, count, one):
    def chunk(c, carry):
        start = first + c * count
        along_z(field, far_z, bands, start + REACH, start, count)
        for r in range(0, count, 2):
            one(start + r)
        return carry

    lax.fori_loop(0, (last - first) // count, chunk, 0)


def along_z(field, far_z, bands, row, i, count):
    v = field[pl.ds(row, count), :, 0:8].reshape(count * BX * 8, 128)
    far_z[pl.ds(i, count)] = band_product(v, bands).reshape(count, BX, 8, 128)


def apply(field, pot, far_z, row, pot_row, i, known=None):
    totals = [[], []]
    for begin in range(0, BX, 4):
        lines = [
            [take(field, row + r, y) for y in range(begin - REACH, begin + 4 + REACH)]
            for r in range(2)
        ]
        for yi in range(begin, begin + 4):
            e = REACH + yi - begin
            x = {0: lines[0][e], 1: lines[1][e]}
            for d in (*range(-REACH, 0), *range(2, REACH + 2)):
                if known is None or row + d in known:
                    x[d] = take(field, row + d, yi)
            for r in range(2):
                line = lines[r]
                total = pot[pot_row + r, yi] * line[e] + far_z[i + r, yi]
                for j in range(1, REACH + 1):
                    near = line[e + j] + line[e - j]
                    beside = [x[d] for d in (r + j, r - j) if d in x]
                    if beside:
                        near = sum(beside[1:], beside[0]) + near
                    total = total + coupling[j] * near
                totals[r].append(total)
    return totals


WHOLE = tuple((8 * z + 2 * k, 8 * z + 2 * k + 4) for z in range(4) for k in range(2))


LOW_SLOTS = ((0, 2), (4, 8), (6, 10))
HIGH_SLOTS = ((0, 4), (2, 6), (8, 10))


def put_pots(pot, sources, slots, row):
    odd = iota((8, 128), 0) % 2 == 1
    for slot, (even_row, odd_row) in enumerate(slots):
        for source, parity in sources:
            for yi in range(BX):
                tile = diagonal + source[slot, yi] * (1.0 / half_width)
                pot[row + even_row + parity, yi] = jnp.where(odd, pltpu.roll(tile, 1, 0), tile)
                pot[row + odd_row + parity, yi] = jnp.where(odd, tile, pltpu.roll(tile, 7, 0))


def steps(field0, field1, field2, pot, far_z):
    def first(i):
        for r, ts in enumerate(apply(field0, pot, far_z, i + REACH, i, i)):
            put(field1, i + r, ts)

    def second(i):
        for r, ts in enumerate(apply(field1, pot, far_z, i + REACH, i + REACH, i)):
            before = i + r + FLAT
            put(field2, i + r, [t + t - take(field0, before, yi) for yi, t in enumerate(ts)])

    return first, second


def inner_kernel(core, got, mid_pot, far_mid, field0, field1, field2, pot, begun, far_z):
    bands = band_parts()
    for z in range(4):
        def fill(xi, carry, z=z):
            put(field0, DEEP + z * BX + xi, [gather(got, z, xi, yi) for yi in range(BX)])
            return carry

        lax.fori_loop(0, BX, fill, 0)
    put_pots(pot, ((mid_pot, core[0]), (far_mid, 1 - core[0])), WHOLE, FLAT)
    first, second = steps(field0, field1, field2, pot, far_z)
    sweep(field0, far_z, bands, *IN1, IN1[1] - IN1[0], first)
    sweep(field1, far_z, bands, *IN2, IN2[1] - IN2[0], second)
    for at, start in enumerate(BEGUN):
        along_z(field0, far_z, bands, start + REACH, start, REACH)
        for r in range(0, REACH, 2):
            i = start + r
            totals = apply(field0, pot, far_z, i + REACH, i, i, OWN)
            for k in range(2):
                for yi in range(BX):
                    begun[at * REACH + r + k, yi] = totals[k][yi]


def pots_kernel(low, high, low_pot, high_pot):
    low_pot[...] = low[DEEP:]
    high_pot[...] = high[DEEP:]


def edge_kernel(core, low, high, _0, _1, field0, pot, far_z):
    bands = band_parts()

    def edge(i, carry):
        put(field0, i, [low[i, yi] for yi in range(BX)])
        put(field0, DEEP + SLAB + i, [high[i, yi] for yi in range(BX)])
        return carry

    lax.fori_loop(0, DEEP, edge, 0)
    put_pots(pot, ((low.at[DEEP:], core[0]),), LOW_SLOTS, 0)
    put_pots(pot, ((high.at[DEEP:], core[0]),), HIGH_SLOTS, FLAT + SLAB)
    along_z(field0, far_z, bands, REACH, 0, FLAT)
    along_z(field0, far_z, bands, REACH + FLAT + SLAB, FLAT + SLAB, FLAT)


def outer_kernel(
    core, far_low, far_high, field0, begun, _1, _2, _3, _4,
    out, field1, field2, pot, far_z,
):
    bands = band_parts()
    put_pots(pot, ((far_low, 1 - core[0]),), LOW_SLOTS, 0)
    put_pots(pot, ((far_high, 1 - core[0]),), HIGH_SLOTS, FLAT + SLAB)
    first, second = steps(field0, field1, field2, pot, far_z)

    def third(i):
        for r, ts in enumerate(apply(field2, pot, far_z, i + REACH, i + FLAT, i)):
            for yi, t in enumerate(ts):
                start = ((i // BX) * 4 * PAIR * BX + i % BX + r) * BX + yi
                out[pl.ds(start, 8, stride=BX * BX), :] = (
                    t + t - take(field1, i + r + FLAT, yi)
                )

    ends1, ends2, half = SLAB + 2 * FLAT, SLAB + FLAT, SLAB // 2

    def rows(one, begin, end):
        for r in range(begin, end, 2):
            one(r)

    def ahead(field, begin, end):
        along_z(field, far_z, bands, begin + REACH, begin, end - begin)

    def complete(at):
        for r in range(REACH):
            i = BEGUN[at] + r
            tiles = []
            for yi in range(BX):
                total = begun[at * REACH + r, yi]
                for j in range(1, REACH + 1):
                    for row in (i + REACH - j, i + REACH + j):
                        if row not in OWN:
                            total = total + coupling[j] * take(field0, row, yi)
                tiles.append(total)
            put(field1, i, tiles)

    rows(first, 0, FLAT), complete(0)
    complete(1), rows(first, FLAT + SLAB, ends1), ahead(field1, 0, IN2[0])
    rows(second, 0, IN2[0]), ahead(field1, IN2[1], ends2)
    rows(second, IN2[1], ends2), ahead(field2, 0, half)
    rows(third, 0, half), ahead(field2, half, SLAB)
    rows(third, half, SLAB)


def iota(shape, dim):
    return lax.broadcasted_iota(jnp.int32, shape, dim)


def spread(orbital_count):
    shape = (orbital_count * BX, orbital_count)
    return (iota(shape, 0) // BX == iota(shape, 1)).astype(jnp.float32)


def same_y(orbital_count):
    shape = (orbital_count * BX, orbital_count * BX)
    return iota(shape, 0) % BX == iota(shape, 1) % BX


def dot(a, b, dims=((1,), (0,))):
    return lax.dot_general(
        a, b, (dims, ((), ())), precision=highest, preferred_element_type=jnp.float32
    )


def pair_of_rows(y, x):
    rows = y.shape[0] * BX
    return jnp.concatenate([y[:, x].reshape(rows, 128), y[:, x + 1].reshape(rows, 128)], axis=1)


def across(a, b):
    return lax.dot_general(a, b, (((1,), (1,)), ((), ())), preferred_element_type=jnp.float32)


def gram_kernel(scale, y, out):
    n = y.shape[0]
    total = None
    for x in range(0, BX, 2):
        high, middle, low = parts_of(pair_of_rows(y, x))
        part = 0.5 * (across(high, high) + across(middle, middle))
        part = part + (across(high, middle) + across(high, low))
        total = part if total is None else total + part
    total = jnp.where(same_y(n), total, 0.0) * scale
    ones = spread(n)
    gram = dot(dot(ones, total, ((0,), (0,))), ones)
    gram = gram + gram.T
    half = n // 2
    upper = iota((half, half), 0) <= iota((half, half), 1)
    kept = jnp.concatenate(
        [jnp.where(upper, gram[:half, :half], gram[half:, half:]), gram[:half, half:]], axis=1
    )
    unit = iota((half, half), 0) == iota((half, half), 1)
    ends = jnp.sum(jnp.where(unit, gram[half:, half:], 0.0), axis=0, keepdims=True)
    ends = jnp.concatenate([ends, jnp.zeros((1, 128 - half), jnp.float32)], axis=1)
    rows = jnp.concatenate([kept[4 * k : 4 * k + 4] for k in range(4)], axis=1)
    rows = jnp.concatenate([rows, ends], axis=0)
    for d in range(out.shape[0] // 5):
        out[5 * d : 5 * d + 5] = rows


def finish_kernel(parts, y2, out, factor):
    n = factor.shape[0]
    half = n // 2
    rows = []
    for r in range(5):
        total = None
        for d in range(0, parts.shape[0] // 5, 8):
            tile = parts[pl.ds(5 * d + r, 8, stride=5), :]
            total = tile if total is None else total + tile
        rows.append(jnp.sum(total, axis=0, keepdims=True))
    rows = jnp.concatenate(rows, axis=0)
    kept = jnp.concatenate([rows[:4, n * k : n * k + n] for k in range(4)], axis=0)
    across = kept[:, half:]
    unit = iota((half, half), 0) == iota((half, half), 1)
    upper = iota((half, half), 0) < iota((half, half), 1)
    mixed = kept[:, :half]
    turned = mixed.T
    first = jnp.where(upper | unit, mixed, turned)
    last = jnp.where(upper, turned, mixed)
    last = jnp.where(unit, jnp.broadcast_to(rows[4:5, :half], (half, half)), last)
    gram = jnp.concatenate(
        [jnp.concatenate([first, across], axis=1), jnp.concatenate([across.T, last], axis=1)],
        axis=0,
    )
    unit = (iota((n, n), 0) == iota((n, n), 1)).astype(jnp.float32)
    left = jnp.concatenate([gram, unit, jnp.zeros((n, 128 - 2 * n), jnp.float32)], axis=1)
    row_of = iota((n, 128), 0)
    finished = []
    for k in range(0, n, STEP):
        entry = {
            (i, j): jnp.broadcast_to(left[k + i : k + i + 1, k + j : k + j + 1], (1, 128))
            for i in range(STEP)
            for j in range(i + 1)
        }
        columns = [
            jnp.broadcast_to(left[:, k + j : k + j + 1], (n, 128)) for j in range(STEP)
        ]
        lines = [left[k + j : k + j + 1] for j in range(STEP)]
        for j in range(STEP):
            inverse = lax.rsqrt(entry[j, j])
            lines[j] = lines[j] * inverse
            columns[j] = columns[j] * inverse
            for i in range(j + 1, STEP):
                entry[i, j] = entry[i, j] * inverse
            for i in range(j + 1, STEP):
                for m in range(j + 1, i + 1):
                    entry[i, m] = entry[i, m] - entry[i, j] * entry[m, j]
                lines[i] = lines[i] - entry[i, j] * lines[j]
                columns[i] = columns[i] - entry[i, j] * columns[j]
        finished += lines
        change = None
        for line, column in zip(lines, columns):
            part = column * line
            change = part if change is None else change + part
        left = jnp.where(row_of >= k + STEP, left - change, left)
    done = jnp.concatenate(finished, axis=0)
    factor[...] = jnp.where(iota((n, n), 0) <= iota((n, n), 1), done[:, :n], 0.0)
    mixer = done[:, n : 2 * n]
    m_high, m_middle, m_low = parts_of(mixer)
    wide = jnp.concatenate([m_high, m_high, m_high, m_middle, m_middle, m_low], axis=1)
    wide = jnp.concatenate([wide, jnp.zeros((n, 256 - 6 * n), jnp.bfloat16)], axis=1)
    for xy in range(0, BX * BX, 2):
        both = []
        for r in range(2):
            both.append(jnp.concatenate([y2[pl.ds(xy + r + 512 * k, 8, stride=64), :] for k in range(n // 8)], axis=0))
        v = jnp.concatenate(both, axis=1)
        high, middle, low = parts_of(v)
        stack = jnp.concatenate([high, middle, low, high, middle, high, jnp.zeros((256 - 6 * n, 256), jnp.bfloat16)], axis=0)
        mixed = jnp.dot(wide, stack, preferred_element_type=jnp.float32)
        for r in range(2):
            for k in range(n // 8):
                out[pl.ds(xy + r + 512 * k, 8, stride=64), :] = mixed[8 * k : 8 * k + 8, 128 * r : 128 * r + 128]


def call(kernel, out_shape, in_specs, scratch=(), limit=8, flops=0, moved=0, aliases={}):
    return pl.pallas_call(
        kernel,
        out_shape=out_shape,
        in_specs=in_specs,
        out_specs=jax.tree.map(lambda _: VMEM, out_shape),
        scratch_shapes=list(scratch),
        input_output_aliases=aliases,
        compiler_params=pltpu.CompilerParams(vmem_limit_bytes=limit << 20),
        cost_estimate=pl.CostEstimate(flops=flops, bytes_accessed=moved, transcendentals=0),
    )


def f32(*shape):
    return jax.ShapeDtypeStruct(shape, jnp.float32)


def per_device(orbitals, potential):
    n = orbitals.shape[0]
    slabs = lax.axis_size("s")
    group = lax.axis_size("z") * lax.axis_size("gy")
    core = lax.axis_index("gy") & 1
    away = pl.BlockSpec(memory_space=pltpu.HBM)
    sent = call(
        message_kernel,
        f32(group, PAIR, BLOCK, BX, 128),
        [away, away],
        [pltpu.VMEM((BX, BX, 128), jnp.float32), pltpu.SemaphoreType.DMA((FLOWS + 1,))],
    )(
        pltpu.with_memory_space_constraint(orbitals.reshape(group, PAIR, BX, BX, 128), pltpu.HBM),
        pltpu.with_memory_space_constraint(potential, pltpu.HBM),
    )
    got = lax.all_to_all(sent, ("z", "gy"), 0, 0, tiled=True)
    got = got.reshape(group * PAIR * BLOCK * BX, 128)
    up, down, mid_pot = call(
        pack_kernel, (f32(DEEP + 3, 8, 8, 128),) * 2 + (f32(8, 8, 8, 128),), [VMEM]
    )(got)
    ring = [(i, (i + 1) % slabs) for i in range(slabs)]
    back_ring = [(j, i) for i, j in ring]
    twin = [(i, i ^ 1) for i in range(lax.axis_size("gy"))]
    low = lax.ppermute(up, "s", ring)
    high = lax.ppermute(down, "s", back_ring)
    far_mid = lax.ppermute(mid_pot, "gy", twin)
    own = (core.reshape(1),)
    fields = tuple(f32(rows, BX, 16, 128) for rows in (SLAB + 2 * DEEP, SLAB + 2 * FLAT, SLAB + FLAT))
    fields += (f32(SLAB + 2 * FLAT, BX, 8, 128),)
    far_z = [pltpu.VMEM((SLAB + 2 * FLAT, BX, 8, 128), jnp.float32)]
    inner = call(inner_kernel, fields + (f32(2 * REACH, BX, 8, 128),), [SMEM] + [VMEM] * 3, far_z, 10, flops=1 << 32)(
        *own, got, mid_pot, far_mid
    )
    low, high, inner = lax.optimization_barrier((low, high, inner))
    low_pot, high_pot = call(pots_kernel, (f32(3, 8, 8, 128),) * 2, [VMEM] * 2)(low, high)
    far_low = lax.ppermute(low_pot, "gy", twin)
    far_high = lax.ppermute(high_pot, "gy", twin)
    field0, field1, field2, pot, begun = inner
    field0, pot, products = call(
        edge_kernel,
        (fields[0], fields[3], fields[3]),
        [SMEM] + [VMEM] * 4,
        (),
        10,
        flops=1 << 30,
        aliases={3: 0, 4: 1},
    )(*own, low, high, field0, pot)
    filtered = call(
        outer_kernel,
        (f32(group * PAIR * BX * BX, 128),) + fields[1:] + (fields[3],),
        [SMEM] + [VMEM] * 8,
        (),
        10,
        aliases={5 + k: 1 + k for k in range(4)},
    )(*own, far_low, far_high, field0, begun, field1, field2, pot, products)[0]
    filtered = filtered.reshape(group, PAIR, BX, BX, 128)
    back = lax.all_to_all(filtered, ("z", "gy"), 0, 0, tiled=True).reshape(n, BX, BX, 128)
    devices = slabs * group
    cells = float(devices * BX * BX * 128)
    parts = call(
        functools.partial(gram_kernel, 1.0 / cells), f32(devices * 5, 128), [VMEM]
    )(back)
    parts = lax.all_to_all(
        parts.reshape(devices, 1, 5 * 128), ("gy", "z", "s"), 0, 0, tiled=True
    ).reshape(devices * 5, 128)
    made, factor = call(finish_kernel, (f32(n * BX * BX, 128), f32(n, n)), [VMEM, VMEM])(
        parts, back.reshape(n * BX * BX, 128)
    )
    return made.reshape(n, BX, BX, 128), factor


def solution(mesh):
    shape = mesh.devices.shape
    fine = Mesh(mesh.devices.reshape(shape[0] // 4, 4, shape[1]), ("s", "z", "gy"))
    return jax.shard_map(
        per_device,
        mesh=fine,
        in_specs=(P(None, ("s", "z"), "gy", None), P(("s", "z"), "gy", None)),
        out_specs=(P(None, ("s", "z"), "gy", None), P()),
        check_vma=False,
    )
```

```python
import functools

import jax
import jax.numpy as jnp
from jax import lax
from jax.experimental import pallas as pl
from jax.experimental.pallas import tpu as pltpu
from jax.sharding import Mesh
from jax.sharding import PartitionSpec as P

stencil_weights = (
    -5369.0 / 1800.0,
    12.0 / 7.0,
    -15.0 / 56.0,
    10.0 / 189.0,
    -1.0 / 112.0,
    2.0 / 1925.0,
    -1.0 / 16632.0,
)
grid_spacing = 0.5
filter_low = 4.0
filter_high = 46.0
centre_shift = 0.5 * (filter_high + filter_low)
half_width = 0.5 * (filter_high - filter_low)
kinetic = -0.5 / grid_spacing**2
diagonal = (kinetic * 3.0 * stencil_weights[0] - centre_shift) / half_width
coupling = tuple(kinetic * w / half_width for w in stencil_weights)
highest = lax.Precision.HIGHEST

REACH = 6
DEEP = 3 * REACH
FLAT = 2 * REACH
FLOWS = 4
STEP = 8
PAIR = 2
IN1 = (DEEP, DEEP + 20)
OWN = range(DEEP, DEEP + 32)
BEGUN = (DEEP - REACH, DEEP + 20)
IN2 = (DEEP, DEEP + 8)
BX = 8
BLOCK = BX + 2
SLAB = 4 * BX
VMEM = pl.BlockSpec(memory_space=pltpu.VMEM)
SMEM = pl.BlockSpec(memory_space=pltpu.SMEM)


def gather(got, z, xi, yi):
    return got[pl.ds(((z * 4) * PAIR * BLOCK + xi) * BX + yi, 8, stride=BLOCK * BX), :]


def message_kernel(orbitals, potential, out, rows, arrived):
    flat = pltpu.make_async_copy(potential, rows, arrived.at[FLOWS])
    flat.start()
    part = out.shape[0] // FLOWS
    copies = []
    for f in range(FLOWS):
        some = pl.ds(f * part, part)
        copies.append(
            pltpu.make_async_copy(orbitals.at[some], out.at[some, :, 0:BX], arrived.at[f])
        )
        copies[-1].start()
    flat.wait()
    for d in range(out.shape[0]):
        for o in range(PAIR):
            for k in range(2):
                out[d, o, BX + k] = rows[4 * o + 2 * k + d % 2]
    for copy in copies:
        copy.wait()


def pack_kernel(got, up, down, mid_pot):
    for dest, first in ((up, SLAB - DEEP), (down, 0)):
        for i in range(DEEP):
            z, xi = divmod(first + i, BX)
            for yi in range(BX):
                dest[i, yi] = gather(got, z, xi, yi)
    odd = iota((8, 128), 0) % 2 == 1
    for yi in range(BX):
        tiles = [[gather(got, z, BX + k, yi) for k in range(2)] for z in range(4)]
        for z in range(4):
            for k in range(2):
                mid_pot[2 * z + k, yi] = tiles[z][k]
        up[DEEP, yi] = jnp.where(odd, tiles[2][1], pltpu.roll(tiles[2][0], 7, 0))
        down[DEEP + 2, yi] = jnp.where(odd, pltpu.roll(tiles[1][1], 1, 0), tiles[1][0])
        for k in range(2):
            up[DEEP + 1 + k, yi] = tiles[3][k]
            down[DEEP + k, yi] = tiles[0][k]


def put(field, row, tiles):
    for yi in range(BX):
        field[row, yi, 0:8] = tiles[yi]
        field[row, yi, 8:16] = tiles[yi]


def take(field, row, yi):
    first = 8 - PAIR if yi < 0 else PAIR if yi >= BX else 0
    return field[row, yi % BX, first : first + 8]


def parts_of(v):
    high = v.astype(jnp.bfloat16)
    rest = v - high.astype(jnp.float32)
    middle = rest.astype(jnp.bfloat16)
    return high, middle, (rest - middle.astype(jnp.float32)).astype(jnp.bfloat16)


def band_parts():
    apart = (iota((128, 128), 0) - iota((128, 128), 1)) % 128
    band = jnp.zeros((128, 128), jnp.float32)
    for j in range(1, REACH + 1):
        band = jnp.where((apart == j) | (apart == 128 - j), coupling[j], band)
    high, middle, low = parts_of(band)
    top = jnp.concatenate([high, middle], axis=1)
    return jnp.concatenate([top, top], axis=0)


def band_product(v, bands):
    high, middle, _ = parts_of(v)
    both = jnp.dot(
        jnp.concatenate([high, middle], axis=1), bands, preferred_element_type=jnp.float32
    )
    return both[:, :128] + both[:, 128:]


def sweep(field, far_z, bands, first, last, count, one):
    def chunk(c, carry):
        start = first + c * count
        along_z(field, far_z, bands, start + REACH, start, count)
        for r in range(0, count, 2):
            one(start + r)
        return carry

    lax.fori_loop(0, (last - first) // count, chunk, 0)


def along_z(field, far_z, bands, row, i, count):
    v = field[pl.ds(row, count), :, 0:8].reshape(count * BX * 8, 128)
    far_z[pl.ds(i, count)] = band_product(v, bands).reshape(count, BX, 8, 128)


def apply(field, pot, far_z, row, pot_row, i, known=None):
    totals = [[], []]
    for begin in range(0, BX, 4):
        lines = [
            [take(field, row + r, y) for y in range(begin - REACH, begin + 4 + REACH)]
            for r in range(2)
        ]
        for yi in range(begin, begin + 4):
            e = REACH + yi - begin
            x = {0: lines[0][e], 1: lines[1][e]}
            for d in (*range(-REACH, 0), *range(2, REACH + 2)):
                if known is None or row + d in known:
                    x[d] = take(field, row + d, yi)
            for r in range(2):
                line = lines[r]
                total = pot[pot_row + r, yi] * line[e] + far_z[i + r, yi]
                for j in range(1, REACH + 1):
                    near = line[e + j] + line[e - j]
                    beside = [x[d] for d in (r + j, r - j) if d in x]
                    if beside:
                        near = sum(beside[1:], beside[0]) + near
                    total = total + coupling[j] * near
                totals[r].append(total)
    return totals


WHOLE = tuple((8 * z + 2 * k, 8 * z + 2 * k + 4) for z in range(4) for k in range(2))


LOW_SLOTS = ((0, 2), (4, 8), (6, 10))
HIGH_SLOTS = ((0, 4), (2, 6), (8, 10))


def put_pots(pot, sources, slots, row):
    odd = iota((8, 128), 0) % 2 == 1
    for slot, (even_row, odd_row) in enumerate(slots):
        for source, parity in sources:
            for yi in range(BX):
                tile = diagonal + source[slot, yi] * (1.0 / half_width)
                pot[row + even_row + parity, yi] = jnp.where(odd, pltpu.roll(tile, 1, 0), tile)
                pot[row + odd_row + parity, yi] = jnp.where(odd, tile, pltpu.roll(tile, 7, 0))


def steps(field0, field1, field2, pot, far_z):
    def first(i):
        for r, ts in enumerate(apply(field0, pot, far_z, i + REACH, i, i)):
            put(field1, i + r, ts)

    def second(i):
        for r, ts in enumerate(apply(field1, pot, far_z, i + REACH, i + REACH, i)):
            before = i + r + FLAT
            put(field2, i + r, [t + t - take(field0, before, yi) for yi, t in enumerate(ts)])

    return first, second


def inner_kernel(core, got, mid_pot, far_mid, field0, field1, field2, pot, begun, far_z):
    bands = band_parts()
    for z in range(4):
        def fill(xi, carry, z=z):
            put(field0, DEEP + z * BX + xi, [gather(got, z, xi, yi) for yi in range(BX)])
            return carry

        lax.fori_loop(0, BX, fill, 0)
    put_pots(pot, ((mid_pot, core[0]), (far_mid, 1 - core[0])), WHOLE, FLAT)
    first, second = steps(field0, field1, field2, pot, far_z)
    sweep(field0, far_z, bands, *IN1, IN1[1] - IN1[0], first)
    sweep(field1, far_z, bands, *IN2, IN2[1] - IN2[0], second)
    for at, start in enumerate(BEGUN):
        along_z(field0, far_z, bands, start + REACH, start, REACH)
        for r in range(0, REACH, 2):
            i = start + r
            totals = apply(field0, pot, far_z, i + REACH, i, i, OWN)
            for k in range(2):
                for yi in range(BX):
                    begun[at * REACH + r + k, yi] = totals[k][yi]


def pots_kernel(low, high, low_pot, high_pot):
    low_pot[...] = low[DEEP:]
    high_pot[...] = high[DEEP:]


def edge_kernel(core, low, high, _0, _1, field0, pot, far_z):
    bands = band_parts()

    def edge(i, carry):
        put(field0, i, [low[i, yi] for yi in range(BX)])
        put(field0, DEEP + SLAB + i, [high[i, yi] for yi in range(BX)])
        return carry

    lax.fori_loop(0, DEEP, edge, 0)
    put_pots(pot, ((low.at[DEEP:], core[0]),), LOW_SLOTS, 0)
    put_pots(pot, ((high.at[DEEP:], core[0]),), HIGH_SLOTS, FLAT + SLAB)
    along_z(field0, far_z, bands, REACH, 0, FLAT)
    along_z(field0, far_z, bands, REACH + FLAT + SLAB, FLAT + SLAB, FLAT)


def outer_kernel(
    core, far_low, far_high, field0, begun, _1, _2, _3, _4,
    out, field1, field2, pot, far_z,
):
    bands = band_parts()
    put_pots(pot, ((far_low, 1 - core[0]),), LOW_SLOTS, 0)
    put_pots(pot, ((far_high, 1 - core[0]),), HIGH_SLOTS, FLAT + SLAB)
    first, second = steps(field0, field1, field2, pot, far_z)

    def third(i):
        for r, ts in enumerate(apply(field2, pot, far_z, i + REACH, i + FLAT, i)):
            for yi, t in enumerate(ts):
                start = ((i // BX) * 4 * PAIR * BX + i % BX + r) * BX + yi
                out[pl.ds(start, 8, stride=BX * BX), :] = (
                    t + t - take(field1, i + r + FLAT, yi)
                )

    ends1, ends2, half = SLAB + 2 * FLAT, SLAB + FLAT, SLAB // 2

    def rows(one, begin, end):
        for r in range(begin, end, 2):
            one(r)

    def ahead(field, begin, end):
        along_z(field, far_z, bands, begin + REACH, begin, end - begin)

    def complete(at):
        for r in range(REACH):
            i = BEGUN[at] + r
            tiles = []
            for yi in range(BX):
                total = begun[at * REACH + r, yi]
                for j in range(1, REACH + 1):
                    for row in (i + REACH - j, i + REACH + j):
                        if row not in OWN:
                            total = total + coupling[j] * take(field0, row, yi)
                tiles.append(total)
            put(field1, i, tiles)

    rows(first, 0, FLAT), complete(0)
    complete(1), rows(first, FLAT + SLAB, ends1), ahead(field1, 0, IN2[0])
    rows(second, 0, IN2[0]), ahead(field1, IN2[1], ends2)
    rows(second, IN2[1], ends2), ahead(field2, 0, half)
    rows(third, 0, half), ahead(field2, half, SLAB)
    rows(third, half, SLAB)


def iota(shape, dim):
    return lax.broadcasted_iota(jnp.int32, shape, dim)


def spread(orbital_count):
    shape = (orbital_count * BX, orbital_count)
    return (iota(shape, 0) // BX == iota(shape, 1)).astype(jnp.float32)


def same_y(orbital_count):
    shape = (orbital_count * BX, orbital_count * BX)
    return iota(shape, 0) % BX == iota(shape, 1) % BX


def dot(a, b, dims=((1,), (0,))):
    return lax.dot_general(
        a, b, (dims, ((), ())), precision=highest, preferred_element_type=jnp.float32
    )


def pair_of_rows(y, x):
    rows = y.shape[0] * BX
    return jnp.concatenate([y[:, x].reshape(rows, 128), y[:, x + 1].reshape(rows, 128)], axis=1)


def across(a, b):
    return lax.dot_general(a, b, (((1,), (1,)), ((), ())), preferred_element_type=jnp.float32)


def gram_kernel(scale, y, out):
    n = y.shape[0]
    total = None
    for x in range(0, BX, 2):
        high, middle, low = parts_of(pair_of_rows(y, x))
        part = 0.5 * (across(high, high) + across(middle, middle))
        part = part + (across(high, middle) + across(high, low))
        total = part if total is None else total + part
    total = jnp.where(same_y(n), total, 0.0) * scale
    ones = spread(n)
    exact = ones.astype(jnp.bfloat16)
    down = (((0,), (0,)), ((), ()))
    tall = sum(
        lax.dot_general(exact, p, down, preferred_element_type=jnp.float32) for p in parts_of(total)
    )
    gram = sum(jnp.dot(p, exact, preferred_element_type=jnp.float32) for p in parts_of(tall))
    gram = gram + gram.T
    half = n // 2
    upper = iota((half, half), 0) <= iota((half, half), 1)
    kept = jnp.concatenate(
        [jnp.where(upper, gram[:half, :half], gram[half:, half:]), gram[:half, half:]], axis=1
    )
    unit = iota((half, half), 0) == iota((half, half), 1)
    ends = jnp.sum(jnp.where(unit, gram[half:, half:], 0.0), axis=0, keepdims=True)
    ends = jnp.concatenate([ends, jnp.zeros((1, 128 - half), jnp.float32)], axis=1)
    rows = jnp.concatenate([kept[4 * k : 4 * k + 4] for k in range(4)], axis=1)
    rows = jnp.concatenate([rows, ends], axis=0)
    for d in range(out.shape[0] // 5):
        out[5 * d : 5 * d + 5] = rows


def finish_kernel(parts, y2, out, factor):
    n = factor.shape[0]
    half = n // 2
    rows = []
    for r in range(5):
        total = None
        for d in range(0, parts.shape[0] // 5, 8):
            tile = parts[pl.ds(5 * d + r, 8, stride=5), :]
            total = tile if total is None else total + tile
        rows.append(jnp.sum(total, axis=0, keepdims=True))
    rows = jnp.concatenate(rows, axis=0)
    kept = jnp.concatenate([rows[:4, n * k : n * k + n] for k in range(4)], axis=0)
    across = kept[:, half:]
    unit = iota((half, half), 0) == iota((half, half), 1)
    upper = iota((half, half), 0) < iota((half, half), 1)
    mixed = kept[:, :half]
    turned = mixed.T
    first = jnp.where(upper | unit, mixed, turned)
    last = jnp.where(upper, turned, mixed)
    last = jnp.where(unit, jnp.broadcast_to(rows[4:5, :half], (half, half)), last)
    gram = jnp.concatenate(
        [jnp.concatenate([first, across], axis=1), jnp.concatenate([across.T, last], axis=1)],
        axis=0,
    )
    unit = (iota((n, n), 0) == iota((n, n), 1)).astype(jnp.float32)
    left = jnp.concatenate([gram, unit, jnp.zeros((n, 128 - 2 * n), jnp.float32)], axis=1)
    row_of = iota((n, 128), 0)
    finished = []
    for k in range(0, n, STEP):
        entry = {
            (i, j): jnp.broadcast_to(left[k + i : k + i + 1, k + j : k + j + 1], (1, 128))
            for i in range(STEP)
            for j in range(i + 1)
        }
        columns = [
            jnp.broadcast_to(left[:, k + j : k + j + 1], (n, 128)) for j in range(STEP)
        ]
        lines = [left[k + j : k + j + 1] for j in range(STEP)]
        for j in range(STEP):
            inverse = lax.rsqrt(entry[j, j])
            lines[j] = lines[j] * inverse
            columns[j] = columns[j] * inverse
            for i in range(j + 1, STEP):
                entry[i, j] = entry[i, j] * inverse
            for i in range(j + 1, STEP):
                for m in range(j + 1, i + 1):
                    entry[i, m] = entry[i, m] - entry[i, j] * entry[m, j]
                lines[i] = lines[i] - entry[i, j] * lines[j]
                columns[i] = columns[i] - entry[i, j] * columns[j]
        finished += lines
        change = None
        for line, column in zip(lines, columns):
            part = column * line
            change = part if change is None else change + part
        left = jnp.where(row_of >= k + STEP, left - change, left)
    done = jnp.concatenate(finished, axis=0)
    factor[...] = jnp.where(iota((n, n), 0) <= iota((n, n), 1), done[:, :n], 0.0)
    mixer = done[:, n : 2 * n]
    m_high, m_middle, m_low = parts_of(mixer)
    wide = jnp.concatenate([m_high, m_high, m_high, m_middle, m_middle, m_low], axis=1)
    wide = jnp.concatenate([wide, jnp.zeros((n, 256 - 6 * n), jnp.bfloat16)], axis=1)
    for xy in range(0, BX * BX, 2):
        both = []
        for r in range(2):
            both.append(jnp.concatenate([y2[pl.ds(xy + r + 512 * k, 8, stride=64), :] for k in range(n // 8)], axis=0))
        v = jnp.concatenate(both, axis=1)
        high, middle, low = parts_of(v)
        stack = jnp.concatenate([high, middle, low, high, middle, high, jnp.zeros((256 - 6 * n, 256), jnp.bfloat16)], axis=0)
        mixed = jnp.dot(wide, stack, preferred_element_type=jnp.float32)
        for r in range(2):
            for k in range(n // 8):
                out[pl.ds(xy + r + 512 * k, 8, stride=64), :] = mixed[8 * k : 8 * k + 8, 128 * r : 128 * r + 128]


def call(kernel, out_shape, in_specs, scratch=(), limit=8, flops=0, moved=0, aliases={}):
    return pl.pallas_call(
        kernel,
        out_shape=out_shape,
        in_specs=in_specs,
        out_specs=jax.tree.map(lambda _: VMEM, out_shape),
        scratch_shapes=list(scratch),
        input_output_aliases=aliases,
        compiler_params=pltpu.CompilerParams(vmem_limit_bytes=limit << 20),
        cost_estimate=pl.CostEstimate(flops=flops, bytes_accessed=moved, transcendentals=0),
    )


def f32(*shape):
    return jax.ShapeDtypeStruct(shape, jnp.float32)


def per_device(orbitals, potential):
    n = orbitals.shape[0]
    slabs = lax.axis_size("s")
    group = lax.axis_size("z") * lax.axis_size("gy")
    core = lax.axis_index("gy") & 1
    away = pl.BlockSpec(memory_space=pltpu.HBM)
    sent = call(
        message_kernel,
        f32(group, PAIR, BLOCK, BX, 128),
        [away, away],
        [pltpu.VMEM((BX, BX, 128), jnp.float32), pltpu.SemaphoreType.DMA((FLOWS + 1,))],
    )(
        pltpu.with_memory_space_constraint(orbitals.reshape(group, PAIR, BX, BX, 128), pltpu.HBM),
        pltpu.with_memory_space_constraint(potential, pltpu.HBM),
    )
    got = lax.all_to_all(sent, ("z", "gy"), 0, 0, tiled=True)
    got = got.reshape(group * PAIR * BLOCK * BX, 128)
    up, down, mid_pot = call(
        pack_kernel, (f32(DEEP + 3, 8, 8, 128),) * 2 + (f32(8, 8, 8, 128),), [VMEM]
    )(got)
    ring = [(i, (i + 1) % slabs) for i in range(slabs)]
    back_ring = [(j, i) for i, j in ring]
    twin = [(i, i ^ 1) for i in range(lax.axis_size("gy"))]
    low = lax.ppermute(up, "s", ring)
    high = lax.ppermute(down, "s", back_ring)
    far_mid = lax.ppermute(mid_pot, "gy", twin)
    own = (core.reshape(1),)
    fields = tuple(f32(rows, BX, 16, 128) for rows in (SLAB + 2 * DEEP, SLAB + 2 * FLAT, SLAB + FLAT))
    fields += (f32(SLAB + 2 * FLAT, BX, 8, 128),)
    far_z = [pltpu.VMEM((SLAB + 2 * FLAT, BX, 8, 128), jnp.float32)]
    inner = call(inner_kernel, fields + (f32(2 * REACH, BX, 8, 128),), [SMEM] + [VMEM] * 3, far_z, 10, flops=1 << 32)(
        *own, got, mid_pot, far_mid
    )
    low, high, inner = lax.optimization_barrier((low, high, inner))
    low_pot, high_pot = call(pots_kernel, (f32(3, 8, 8, 128),) * 2, [VMEM] * 2)(low, high)
    far_low = lax.ppermute(low_pot, "gy", twin)
    far_high = lax.ppermute(high_pot, "gy", twin)
    field0, field1, field2, pot, begun = inner
    field0, pot, products = call(
        edge_kernel,
        (fields[0], fields[3], fields[3]),
        [SMEM] + [VMEM] * 4,
        (),
        10,
        flops=1 << 30,
        aliases={3: 0, 4: 1},
    )(*own, low, high, field0, pot)
    filtered = call(
        outer_kernel,
        (f32(group * PAIR * BX * BX, 128),) + fields[1:] + (fields[3],),
        [SMEM] + [VMEM] * 8,
        (),
        10,
        aliases={5 + k: 1 + k for k in range(4)},
    )(*own, far_low, far_high, field0, begun, field1, field2, pot, products)[0]
    filtered = filtered.reshape(group, PAIR, BX, BX, 128)
    back = lax.all_to_all(filtered, ("z", "gy"), 0, 0, tiled=True).reshape(n, BX, BX, 128)
    devices = slabs * group
    cells = float(devices * BX * BX * 128)
    parts = call(
        functools.partial(gram_kernel, 1.0 / cells), f32(devices * 5, 128), [VMEM]
    )(back)
    parts = lax.all_to_all(
        parts.reshape(devices, 1, 5 * 128), ("gy", "z", "s"), 0, 0, tiled=True
    ).reshape(devices * 5, 128)
    made, factor = call(finish_kernel, (f32(n * BX * BX, 128), f32(n, n)), [VMEM, VMEM])(
        parts, back.reshape(n * BX * BX, 128)
    )
    return made.reshape(n, BX, BX, 128), factor


def solution(mesh):
    shape = mesh.devices.shape
    fine = Mesh(mesh.devices.reshape(shape[0] // 4, 4, shape[1]), ("s", "z", "gy"))
    return jax.shard_map(
        per_device,
        mesh=fine,
        in_specs=(P(None, ("s", "z"), "gy", None), P(("s", "z"), "gy", None)),
        out_specs=(P(None, ("s", "z"), "gy", None), P()),
        check_vma=False,
    )
```
